256 devices in a mesh: pb: 16 (over x_lo, z), ka: 16 (over x_hi, y, core).
Axes of the slice: x: 4 (x_hi: 2, x_lo: 2; x = x_hi * 2 + x_lo), y: 4, z: 8, core: 2. Of those that a mesh axis runs over, the one named last changes fastest.
Arguments:
- query_saved: bfloat16 [8192, 1024], P(('pb', 'ka')), may hold values from -6 to 6
- key_saved: bfloat16 [16384, 1024], P(('ka', 'pb')), may hold values from -6 to 6
- value_saved: bfloat16 [16384, 1024], P(('ka', 'pb')), may hold values from -6 to 6
- out_grad: bfloat16 [8192, 1024], P(('pb', 'ka')), may hold values from -768 to 768
- log_norm: bfloat16 [16, 8192], P(None, ('pb', 'ka')), as said below
- row_delta: bfloat16 [16, 8192], P(None, ('pb', 'ka')), may hold values from -1536 to 1536
- weight_query: bfloat16 [1024, 1024], replicated, may hold values from -0.1875 to 0.1875
- weight_key: bfloat16 [1024, 1024], replicated, may hold values from -0.1875 to 0.1875
- weight_value: bfloat16 [1024, 1024], replicated, may hold values from -0.1875 to 0.1875
Outputs:
- dx_query: bfloat16 [8192, 1024], P(('pb', 'ka'))
- dx_keyvalue: bfloat16 [16384, 1024], P(('ka', 'pb'))
The draws below stay inside these ranges and needn't reach their ends.
Inputs may be any that keep to these rules, and one draw needn't show every extreme that they name: `log_norm`: each entry lies within 2 of 0.5 plus the natural logarithm of 16384.
All inputs are finite; a program needn't handle non-finite values.
Results may differ from the reference program's by a relative error of at most 0.008.
Values may be sent and summed in bfloat16 or wider, within the bound.
A program may use at most 128 MiB of HBM per device.

```python
import jax
import jax.numpy as jnp
from jax import lax

D = 1024
HEAD_DIM = 64
QTOK_DEV = 32
HEADS = 16
TOKENS = 16384
QUERIES = 8192
N_KA = 16


def draw_log_norm(key, part):
    jitter = jax.random.uniform(key, (HEADS, QUERIES), jnp.float32, -1.0, 1.0)
    return (jnp.log(jnp.float32(TOKENS)) + 0.5 + jitter).astype(jnp.bfloat16)


def level_of(stream_key, shape, split, smallest, top_value):
    loudness = 1.0
    for dim, parts in split:
        draws = jax.random.uniform(jax.random.fold_in(jax.random.fold_in(stream_key, 6), dim), (parts,), jnp.float32, smallest / len(split), top_value / len(split))
        loudness = loudness * jnp.repeat(jnp.exp(draws), shape[dim] // parts).reshape((-1,) + (1,) * (len(shape) - 1 - dim))
    return loudness


def scatter_about(own_key, extent, scale, most, shards=(), held_as=jnp.bfloat16):
    entries = scale * jax.random.normal(own_key, extent, jnp.float32)
    if shards:
        entries = entries * level_of(own_key, extent, shards, -0.22, 0.18)
    return jnp.clip(entries, -most, most).astype(held_as)


def setup_inputs(seed: int = 0) -> dict:
    splits = jax.random.split(jax.random.key(seed), 10)
    query_saved = scatter_about(splits[0], (QUERIES, D), 1.0, 6.0, ((0, 256),))
    key_saved = scatter_about(splits[1], (TOKENS, D), 1.0, 6.0, ((0, 256),))
    value_saved = scatter_about(splits[2], (TOKENS, D), 1.0, 6.0, ((0, 256),))
    out_grad = scatter_about(splits[3], (QUERIES, D), 128.0, 768.0, ((0, 256),))
    log_norm = draw_log_norm(jax.random.fold_in(splits[9], 71), 0)
    row_delta = scatter_about(splits[5], (HEADS, QUERIES), 256.0, 1536.0, ((1, 256),))
    weight_query = scatter_about(splits[6], (D, D), D ** -0.5, 0.1875)
    weight_key = scatter_about(splits[7], (D, D), D ** -0.5, 0.1875)
    weight_value = scatter_about(splits[8], (D, D), D ** -0.5, 0.1875)
    return {"query_saved": query_saved, "key_saved": key_saved, "value_saved": value_saved, "out_grad": out_grad, "log_norm": log_norm, "row_delta": row_delta, "weight_query": weight_query, "weight_key": weight_key, "weight_value": weight_value}


def reference(query_saved, key_saved, value_saved, out_grad, log_norm, row_delta, weight_query, weight_key, weight_value):
    query_total = query_saved.shape[0]
    key_total = key_saved.shape[0]
    block_rows = QTOK_DEV * N_KA
    blocks = query_total // block_rows
    head_count = D // HEAD_DIM
    score_scale = 1.0 / (HEAD_DIM ** 0.5)

    def per_head(head_index):
        column = head_index * HEAD_DIM
        queries = lax.dynamic_slice_in_dim(query_saved, column, HEAD_DIM, 1)
        keys_head = lax.dynamic_slice_in_dim(key_saved, column, HEAD_DIM, 1)
        values_head = lax.dynamic_slice_in_dim(value_saved, column, HEAD_DIM, 1)
        grads_head = lax.dynamic_slice_in_dim(out_grad, column, HEAD_DIM, 1)
        norm_row = lax.dynamic_index_in_dim(log_norm, head_index, 0, keepdims=False).astype(jnp.float32)
        delta_row = lax.dynamic_index_in_dim(row_delta, head_index, 0, keepdims=False).astype(jnp.float32)

        def query_step(totals, block_index):
            grad_key, grad_value = totals
            first_row = (block_index * block_rows).astype(jnp.int32)
            query_block = lax.dynamic_slice_in_dim(queries, first_row, block_rows, 0)
            grad_block = lax.dynamic_slice_in_dim(grads_head, first_row, block_rows, 0)
            norm_block = lax.dynamic_slice_in_dim(norm_row, first_row, block_rows, 0)
            delta_block = lax.dynamic_slice_in_dim(delta_row, first_row, block_rows, 0)
            scores = jnp.dot(query_block, keys_head.T, preferred_element_type=jnp.float32) * score_scale
            probs = jnp.exp(scores - norm_block[:, None])
            probs_b = probs.astype(jnp.bfloat16)
            grad_probs = jnp.dot(grad_block, values_head.T, preferred_element_type=jnp.float32)
            grad_scores = probs * (grad_probs - delta_block[:, None])
            grad_scores_b = grad_scores.astype(jnp.bfloat16)
            grad_value = grad_value + jnp.dot(probs_b.T, grad_block, preferred_element_type=jnp.float32)
            grad_key = grad_key + jnp.dot(grad_scores_b.T, query_block, preferred_element_type=jnp.float32) * score_scale
            grad_query = jnp.dot(grad_scores_b, keys_head, preferred_element_type=jnp.float32) * score_scale
            return (grad_key, grad_value), grad_query

        start_totals = (jnp.zeros((key_total, HEAD_DIM), jnp.float32), jnp.zeros((key_total, HEAD_DIM), jnp.float32))
        (grad_key, grad_value), query_parts = lax.scan(query_step, start_totals, jnp.arange(blocks, dtype=jnp.int32))
        return query_parts.reshape(query_total, HEAD_DIM), grad_key, grad_value

    grad_query, grad_key, grad_value = lax.map(per_head, jnp.arange(head_count, dtype=jnp.int32))

    def merge_heads(stacked, row_count):
        return jnp.transpose(stacked, (1, 0, 2)).reshape(row_count, D)

    grad_query = merge_heads(grad_query, query_total)
    grad_key = merge_heads(grad_key, key_total)
    grad_value = merge_heads(grad_value, key_total)
    contract = (((1,), (1,)), ((), ()))

    def project(grads, weights):
        return lax.dot_general(grads, weights.astype(jnp.float32), contract, precision=lax.Precision.HIGHEST, preferred_element_type=jnp.float32)

    dx_query = project(grad_query, weight_query).astype(jnp.bfloat16)
    dx_keyvalue = (project(grad_key, weight_key) + project(grad_value, weight_value)).astype(jnp.bfloat16)
    return (dx_query, dx_keyvalue)
```

```python
import jax
import jax.numpy as jnp
from jax import lax
from jax.experimental import pallas as pl
from jax.experimental.pallas import tpu as pltpu
from jax.sharding import PartitionSpec as P

NX, NY, NZ, NC = 4, 4, 8, 2
PAIRS = NX * NC
LANES = 128
Q_OWN, K_OWN = 32, 64
Q_PART, K_PART = Q_OWN * PAIRS, K_OWN * PAIRS
Q_ALL, K_ALL = Q_PART * NZ, K_PART * NY
TQ, TK = 512, 1024
BF, F32 = jnp.bfloat16, jnp.float32
NT = (((1,), (1,)), ((), ()))
NN = (((1,), (0,)), ((), ()))
TN = (((0,), (0,)), ((), ()))
OTHERS = [(dx, dc) for dx in range(NX) for dc in range(NC) if dx or dc]


def dot(a, b, dims):
    return lax.dot_general(a, b, dims, preferred_element_type=F32)


def rows(start, size):
    return pl.ds(pl.multiple_of(start, size), size)


def kernel(
    q_hbm, k_hbm, v_hbm, g_hbm, norm, delta, wq_hbm, wk_hbm, wv_hbm,
    out_q, out_kv,
    q, g, k, v, aux_out, aux_in, aux,
    qm, gm, an, ad, kt, dqt, dk, dv,
    send_q, send_kv, got_q, got_kv, sum_q, sum_kv, full_q, full_k, full_v,
    wq, wk, wv,
    a_send, a_recv, own_sem, w_sem, z_send, z_recv, y_send, y_recv,
    rq_send, rq_recv, rkv_send, rkv_recv, b_send, b_recv, bown_sem,
):
    pb, ka = lax.axis_index("pb"), lax.axis_index("ka")
    z, y, c = pb % NZ, (ka // NC) % NY, ka % NC
    x = (ka // (NC * NY)) * 2 + pb // NZ
    me = x * NC + c

    def at(x, y, z, c):
        return {"pb": (x % 2) * NZ + z, "ka": (x // 2) * (NY * NC) + y * NC + c}

    def side(dx, dc):
        return at((x + dx) % NX, y, z, (c + dc) % NC)

    def up_z(dz):
        return at(x, y, (z + dz) % NZ, c)

    def up_y(dy):
        return at(x, (y + dy) % NY, z, c)

    def remote(src, dst, send, recv, device):
        return pltpu.make_async_remote_copy(
            src_ref=src, dst_ref=dst, send_sem=send, recv_sem=recv,
            device_id=device, device_id_type=pl.DeviceIdType.MESH,
        )

    peers = [side(dx, dc) for dx, dc in OTHERS]
    peers += [up_z(dz) for dz in range(1, NZ)] + [up_y(dy) for dy in range(1, NY)]
    barrier = pltpu.get_barrier_semaphore()
    for peer in peers:
        pl.semaphore_signal(barrier, inc=1, device_id=peer, device_id_type=pl.DeviceIdType.MESH)
    pl.semaphore_wait(barrier, len(peers))

    my_q = rows(z * Q_PART + me * Q_OWN, Q_OWN)
    my_k = rows(y * K_PART + me * K_OWN, K_OWN)
    sends = []
    for dx, dc in OTHERS:
        j = dx * NC + dc
        cols = rows(((x + dx) % NX * NC + (c + dc) % NC) * LANES, LANES)
        for i, (src, dst, at_rows) in enumerate(
            [(q_hbm, q, my_q), (g_hbm, g, my_q), (k_hbm, k, my_k), (v_hbm, v, my_k)]
        ):
            copy = remote(
                src.at[:, cols], dst.at[at_rows, :], a_send.at[i, j], a_recv.at[i, j], side(dx, dc)
            )
            copy.start()
            sends.append(copy)
    cols = rows(me * LANES, LANES)
    own = []
    for i, (src, dst, at_rows) in enumerate(
        [(q_hbm, q, my_q), (g_hbm, g, my_q), (k_hbm, k, my_k), (v_hbm, v, my_k)]
    ):
        copy = pltpu.make_async_copy(src.at[:, cols], dst.at[at_rows, :], own_sem.at[i])
        copy.start()
        own.append(copy)
    row = lax.broadcasted_iota(jnp.int32, (NX * NC * 2, PAIRS * LANES), 0)
    lane = lax.broadcasted_iota(jnp.int32, (NX * NC * 2, PAIRS * LANES), 1)
    same_pair = lane // LANES == row // 2
    pick = lambda first: jnp.where(
        jnp.logical_and(same_pair, lane % LANES == 4 * me + first + row % 2), -1.0, 0.0
    ).astype(BF)
    aux_out[...] = (dot(norm[...], pick(0), TN) + dot(delta[...], pick(2), TN)).astype(BF)
    for dx, dc in OTHERS:
        j = dx * NC + dc
        cols = rows(((x + dx) % NX * NC + (c + dc) % NC) * LANES, LANES)
        copy = remote(
            aux_out.at[:, cols], aux_in.at[j], a_send.at[4, j], a_recv.at[4, j], side(dx, dc)
        )
        copy.start()
        sends.append(copy)
    weights = []
    for i, (src, dst) in enumerate([(wq_hbm, wq), (wk_hbm, wk), (wv_hbm, wv)]):
        copy = pltpu.make_async_copy(src, dst, w_sem.at[i])
        copy.start()
        weights.append(copy)
    aux_sum = aux_out[:, rows(me * LANES, LANES)].astype(F32)
    for copy in own:
        copy.wait()
    for copy in sends:
        copy.wait()
    for dx, dc in OTHERS:
        aux_sum += aux_in[dx * NC + dc].astype(F32)
    aux[z] = aux_sum.astype(BF)

    def pass_on(step):
        moves = []
        if step <= NZ // 2:
            right, left = (z - step + 1 + NZ) % NZ, (z + step - 1) % NZ
            half = step == NZ // 2
            for i, buf in enumerate([q, g]):
                for d, (origin, to) in enumerate([(right, up_z(1)), (left, up_z(NZ - 1))]):
                    if half and i != d:
                        continue
                    part = buf.at[rows(origin * Q_PART, Q_PART), :]
                    moves.append(remote(
                        part, part, z_send.at[i, d, step - 1], z_recv.at[i, d, step - 1], to
                    ))
            for d, (origin, to) in enumerate([(right, up_z(1)), (left, up_z(NZ - 1))]):
                if half and d:
                    continue
                moves.append(remote(
                    aux.at[origin], aux.at[origin],
                    z_send.at[2, d, step - 1], z_recv.at[2, d, step - 1], to,
                ))
        if step <= NY // 2:
            right, left = (y - step + 1 + NY) % NY, (y + step - 1) % NY
            half = step == NY // 2
            for i, buf in enumerate([k, v]):
                for d, (origin, to) in enumerate([(right, up_y(1)), (left, up_y(NY - 1))]):
                    if half and i != d:
                        continue
                    part = buf.at[rows(origin * K_PART, K_PART), :]
                    moves.append(remote(
                        part, part, y_send.at[i, d, step - 1], y_recv.at[i, d, step - 1], to
                    ))
        return moves

    for step in range(1, NZ // 2 + 1):
        moves = pass_on(step)
        for copy in moves:
            copy.start()
        for copy in moves:
            copy.wait()

    lane = lax.broadcasted_iota(jnp.int32, (Q_PART, LANES), 1)
    row = lax.broadcasted_iota(jnp.int32, (Q_PART, LANES), 0)

    def prepare_q(part, _):
        at_rows = rows(part * Q_PART, Q_PART)
        queries = q[at_rows, :].astype(F32) * 0.125
        grads = g[at_rows, :].astype(F32)
        columns = jnp.concatenate([aux[part].astype(F32)] * PAIRS, axis=0)
        mine = lane // 4 == row // Q_OWN
        for h in range(2):
            head = lane // 64 == h
            qm[h, at_rows, :] = jnp.where(head, queries, 0.0).astype(BF)
            gm[h, at_rows, :] = jnp.where(head, grads, 0.0).astype(BF)
            for dst, first in [(an, 0), (ad, 2)]:
                keep = jnp.logical_and(mine, lane % 4 == first + h)
                dst[h, at_rows, :] = jnp.where(keep, columns, 0.0).astype(BF)
        return 0

    lax.fori_loop(0, NZ, prepare_q, 0)

    def prepare_k(part, _):
        at_rows = rows(part * K_PART, K_PART)
        kt[:, at_rows] = (k[at_rows, :].astype(F32) * 0.125).T.astype(BF)
        return 0

    lax.fori_loop(0, NY, prepare_k, 0)
    dk[...] = jnp.zeros_like(dk)
    dv[...] = jnp.zeros_like(dv)
    dqt[...] = jnp.zeros_like(dqt)
    ones = jnp.ones((TK, LANES), BF)

    def tile(i, _):
        at_q, at_k = rows(i // (K_ALL // TK) * TQ, TQ), rows(i % (K_ALL // TK) * TK, TK)
        keys = jnp.concatenate([k[at_k, :], ones], axis=1)
        values = jnp.concatenate([v[at_k, :], ones], axis=1)
        grad_v = grad_k = None
        for h in range(2):
            scores = dot(keys, jnp.concatenate([qm[h, at_q, :], an[h, at_q, :]], axis=1), NT)
            grads = dot(values, jnp.concatenate([gm[h, at_q, :], ad[h, at_q, :]], axis=1), NT)
            probs = jnp.exp(scores)
            grad_scores = (probs * grads).astype(BF)
            part_v = dot(probs.astype(BF), gm[h, at_q, :], NN)
            part_k = dot(grad_scores, qm[h, at_q, :], NN)
            grad_v = part_v if grad_v is None else grad_v + part_v
            grad_k = part_k if grad_k is None else grad_k + part_k
            head = pl.ds(h * 64, 64)
            dqt[head, at_q] += dot(kt[head, at_k], grad_scores, NN)
        dv[at_k, :] += grad_v
        dk[at_k, :] += grad_k
        return 0

    lax.fori_loop(0, (Q_ALL // TQ) * (K_ALL // TK), tile, 0)

    def pack_q(part, _):
        at_rows = rows(part * Q_PART, Q_PART)
        send_q[at_rows, :] = dqt[:, at_rows].T.astype(BF)
        return 0

    lax.fori_loop(0, NZ, pack_q, 0)
    send_kv[:, :LANES] = dk[...].astype(BF)
    send_kv[:, LANES:] = dv[...].astype(BF)
    moves = []
    for dy in range(1, NY):
        to = (y + dy) % NY
        moves.append(remote(
            send_kv.at[rows(to * K_PART, K_PART), :], got_kv.at[dy - 1],
            rkv_send.at[dy - 1], rkv_recv.at[dy - 1], up_y(dy),
        ))
    for dz in range(1, NZ):
        to = (z + dz) % NZ
        moves.append(remote(
            send_q.at[rows(to * Q_PART, Q_PART), :], got_q.at[dz - 1],
            rq_send.at[dz - 1], rq_recv.at[dz - 1], up_z(dz),
        ))
    for copy in moves:
        copy.start()
    for copy in moves:
        copy.wait()
    total = send_q[rows(z * Q_PART, Q_PART), :].astype(F32)
    for i in range(NZ - 1):
        total += got_q[i].astype(F32)
    sum_q[...] = total.astype(BF)
    total = send_kv[rows(y * K_PART, K_PART), :].astype(F32)
    for i in range(NY - 1):
        total += got_kv[i].astype(F32)
    sum_kv[...] = total.astype(BF)

    cols = rows(me * LANES, LANES)
    moves = []
    for dx, dc in OTHERS:
        j = dx * NC + dc
        to = (x + dx) % NX * NC + (c + dc) % NC
        at_q, at_k = rows(to * Q_OWN, Q_OWN), rows(to * K_OWN, K_OWN)
        for i, (src, dst) in enumerate([
            (sum_q.at[at_q, :], full_q),
            (sum_kv.at[at_k, pl.ds(0, LANES)], full_k),
            (sum_kv.at[at_k, pl.ds(LANES, LANES)], full_v),
        ]):
            moves.append(remote(
                src, dst.at[:, cols], b_send.at[i, j], b_recv.at[i, j], side(dx, dc)
            ))
    at_q, at_k = rows(me * Q_OWN, Q_OWN), rows(me * K_OWN, K_OWN)
    for i, (src, dst) in enumerate([
        (sum_q.at[at_q, :], full_q),
        (sum_kv.at[at_k, pl.ds(0, LANES)], full_k),
        (sum_kv.at[at_k, pl.ds(LANES, LANES)], full_v),
    ]):
        moves.append(pltpu.make_async_copy(src, dst.at[:, cols], bown_sem.at[i]))
    for copy in moves:
        copy.start()
    for copy in weights:
        copy.wait()
    for copy in moves:
        copy.wait()
    out_q[...] = dot(full_q[...], wq[...], NT).astype(BF)
    out_kv[...] = (dot(full_k[...], wk[...], NT) + dot(full_v[...], wv[...], NT)).astype(BF)


def local(query_saved, key_saved, value_saved, out_grad, log_norm, row_delta, wq, wk, wv):
    width = query_saved.shape[1]
    hbm, vmem = pl.BlockSpec(memory_space=pl.ANY), pl.BlockSpec(memory_space=pltpu.VMEM)
    dma = pltpu.SemaphoreType.DMA
    return pl.pallas_call(
        kernel,
        out_shape=(
            jax.ShapeDtypeStruct((Q_OWN, width), BF),
            jax.ShapeDtypeStruct((K_OWN, width), BF),
        ),
        in_specs=[hbm] * 4 + [vmem] * 2 + [hbm] * 3,
        out_specs=(vmem, vmem),
        scratch_shapes=[
            pltpu.VMEM((Q_ALL, LANES), BF), pltpu.VMEM((Q_ALL, LANES), BF),
            pltpu.VMEM((K_ALL, LANES), BF), pltpu.VMEM((K_ALL, LANES), BF),
            pltpu.VMEM((Q_OWN, width), BF), pltpu.VMEM((PAIRS, Q_OWN, LANES), BF),
            pltpu.VMEM((NZ, Q_OWN, LANES), BF),
            *[pltpu.VMEM((2, Q_ALL, LANES), BF)] * 4,
            pltpu.VMEM((LANES, K_ALL), BF), pltpu.VMEM((LANES, Q_ALL), F32),
            pltpu.VMEM((K_ALL, LANES), F32), pltpu.VMEM((K_ALL, LANES), F32),
            pltpu.VMEM((Q_ALL, LANES), BF), pltpu.VMEM((K_ALL, 2 * LANES), BF),
            pltpu.VMEM((NZ - 1, Q_PART, LANES), BF), pltpu.VMEM((NY - 1, K_PART, 2 * LANES), BF),
            pltpu.VMEM((Q_PART, LANES), BF), pltpu.VMEM((K_PART, 2 * LANES), BF),
            pltpu.VMEM((Q_OWN, width), BF), pltpu.VMEM((K_OWN, width), BF),
            pltpu.VMEM((K_OWN, width), BF),
            *[pltpu.VMEM((width, width), BF)] * 3,
            dma((5, PAIRS)), dma((5, PAIRS)), dma((4,)), dma((3,)),
            dma((3, 2, NZ // 2)), dma((3, 2, NZ // 2)), dma((2, 2, NY // 2)), dma((2, 2, NY // 2)),
            dma((NZ - 1,)), dma((NZ - 1,)), dma((NY - 1,)), dma((NY - 1,)),
            dma((3, PAIRS)), dma((3, PAIRS)), dma((3,)),
        ],
        compiler_params=pltpu.CompilerParams(
            collective_id=0, has_side_effects=True, vmem_limit_bytes=60 * 2**20
        ),
        name="attention_backward",
    )(query_saved, key_saved, value_saved, out_grad, log_norm, row_delta, wq, wk, wv)


def solution(mesh):
    in_specs = (
        P(("pb", "ka"), None),
        P(("ka", "pb"), None),
        P(("ka", "pb"), None),
        P(("pb", "ka"), None),
        P(None, ("pb", "ka")),
        P(None, ("pb", "ka")),
        P(),
        P(),
        P(),
    )
    out_specs = (P(("pb", "ka"), None), P(("ka", "pb"), None))
    return jax.shard_map(local, mesh=mesh, in_specs=in_specs, out_specs=out_specs, check_vma=False)
```

```python
import jax
import jax.numpy as jnp
from jax import lax
from jax.experimental import pallas as pl
from jax.experimental.pallas import tpu as pltpu
from jax.sharding import PartitionSpec as P

NX, NY, NZ, NC = 4, 4, 8, 2
PAIRS = NX * NC
LANES = 128
Q_OWN, K_OWN = 32, 64
Q_PART, K_PART = Q_OWN * PAIRS, K_OWN * PAIRS
Q_ALL, K_ALL = Q_PART * NZ, K_PART * NY
BF, F32 = jnp.bfloat16, jnp.float32
NT = (((1,), (1,)), ((), ()))
NN = (((1,), (0,)), ((), ()))
TN = (((0,), (0,)), ((), ()))
MESH = pl.DeviceIdType.MESH
OTHERS = [(dx, dc) for dx in range(NX) for dc in range(NC) if dx or dc]


def dot(a, b, dims):
    return lax.dot_general(a, b, dims, preferred_element_type=F32)


def rows(start, size):
    return pl.ds(pl.multiple_of(start, size), size)


def kernel(
    q_hbm, k_hbm, v_hbm, g_hbm, norm, delta, wq_hbm, wk_hbm, wv_hbm,
    out_q, out_kv,
    q, g, k, v, aux_out, aux_in, aux,
    qm, gm, qr, an, ad, kt, dqt, acc,
    send_q, send_kv, got_q, got_kv, sum_q, sum_kv, full_q, full_k, full_v,
    wq, wk, wv,
    a_send, a_recv, own_sem, w_sem, z1_send, z1_recv, y1_send, y1_recv,
    z_send, z_recv, y_send, y_recv,
    rq_send, rq_recv, rkv_send, rkv_recv, b_send, b_recv, bown_sem,
):
    pb, ka = lax.axis_index("pb"), lax.axis_index("ka")
    z, y, c = pb % NZ, (ka // NC) % NY, ka % NC
    x = (ka // (NC * NY)) * 2 + pb // NZ
    me = x * NC + c

    def at(x, y, z, c):
        return {"pb": (x % 2) * NZ + z, "ka": (x // 2) * (NY * NC) + y * NC + c}

    def side(dx, dc):
        return at((x + dx) % NX, y, z, (c + dc) % NC)

    def ring(here, place, size):
        return (here + (place + 1) // 2 * (place % 2 * 2 - 1) + size) % size

    def z_at(place):
        return ring(z, place, NZ)

    def y_at(place):
        return ring(y, place, NY)

    def to_z(z):
        return at(x, y, z, c)

    def to_y(y):
        return at(x, y, z, c)

    def remote(src, dst, send, recv, device):
        return pltpu.make_async_remote_copy(
            src_ref=src, dst_ref=dst, send_sem=send, recv_sem=recv,
            device_id=device, device_id_type=MESH,
        )

    peers = [side(dx, dc) for dx, dc in OTHERS]
    peers += [to_z(z_at(i)) for i in range(1, NZ)] + [to_y(y_at(i)) for i in range(1, NY)]
    barrier = pltpu.get_barrier_semaphore()
    for peer in peers:
        pl.semaphore_signal(barrier, inc=1, device_id=peer, device_id_type=MESH)

    my_q = rows(z * Q_PART + me * Q_OWN, Q_OWN)
    my_k = rows(y * K_PART + me * K_OWN, K_OWN)
    exchanged = [(q_hbm, q, my_q), (g_hbm, g, my_q), (k_hbm, k, my_k), (v_hbm, v, my_k)]
    mine = rows(me * LANES, LANES)
    own = [
        pltpu.make_async_copy(src.at[:, mine], dst.at[at_rows, :], own_sem.at[i])
        for i, (src, dst, at_rows) in enumerate(exchanged)
    ]
    for copy in own:
        copy.start()
    row = lax.broadcasted_iota(jnp.int32, (NX * NC * 2, PAIRS * LANES), 0)
    lane = lax.broadcasted_iota(jnp.int32, (NX * NC * 2, PAIRS * LANES), 1)
    same_pair = lane // LANES == row // 2
    pick = lambda first: jnp.where(
        jnp.logical_and(same_pair, lane % LANES == 4 * me + first + row % 2), -1.0, 0.0
    ).astype(BF)
    aux_out[...] = (dot(norm[...], pick(0), TN) + dot(delta[...], pick(2), TN)).astype(BF)
    acc[...] = jnp.zeros_like(acc)
    dqt[...] = jnp.zeros_like(dqt)
    pl.semaphore_wait(barrier, len(peers))

    sent = []
    arrivals = {}
    for dx in (1, 3, 2, 0):
        arrivals[dx] = []
        for dc in range(NC):
            if not (dx or dc):
                continue
            j = dx * NC + dc
            cols = rows(((x + dx) % NX * NC + (c + dc) % NC) * LANES, LANES)
            moves = [
                remote(src.at[:, cols], dst.at[at_rows, :], a_send.at[i, j], a_recv.at[i, j], side(dx, dc))
                for i, (src, dst, at_rows) in enumerate(exchanged)
            ]
            moves.append(remote(
                aux_out.at[:, cols], aux_in.at[j], a_send.at[4, j], a_recv.at[4, j], side(dx, dc)
            ))
            for copy in moves:
                copy.start()
            sent += moves
            arrivals[dx] += moves
    weights = [
        pltpu.make_async_copy(src, dst, w_sem.at[i])
        for i, (src, dst) in enumerate([(wq_hbm, wq), (wk_hbm, wk), (wv_hbm, wv)])
    ]

    z_ways = [to_z(z_at(1)), to_z(z_at(2))]
    y_ways = [to_y(y_at(1)), to_y(y_at(2))]
    first_z, first_y = [], []
    for copy in own:
        copy.wait()
    for dx in (0, 1, 3, 2):
        for copy in arrivals[dx]:
            copy.wait_recv()
        from_x = (x - dx + NX) % NX
        at_q = rows(z * Q_PART + from_x * NC * Q_OWN, NC * Q_OWN)
        at_k = rows(y * K_PART + from_x * NC * K_OWN, NC * K_OWN)
        for d in range(2):
            for i, buf in enumerate([q, g]):
                part = buf.at[at_q, :]
                first_z.append(remote(part, part, z1_send.at[i, d, dx], z1_recv.at[i, d, dx], z_ways[d]))
                first_z[-1].start()
            for i, buf in enumerate([k, v]):
                part = buf.at[at_k, :]
                first_y.append(remote(part, part, y1_send.at[i, d, dx], y1_recv.at[i, d, dx], y_ways[d]))
                first_y[-1].start()
    aux_sum = aux_out[:, mine].astype(F32)
    for dx, dc in OTHERS:
        aux_sum += aux_in[dx * NC + dc].astype(F32)
    aux[z] = aux_sum.astype(BF)

    def hop_z(step):
        moves = []
        origins = [(z - step + 1 + NZ) % NZ, (z + step - 1) % NZ]
        for i, buf in enumerate([q, g, aux]):
            if step == 1 and i < 2:
                continue
            for d in range(2):
                if step == NZ // 2 and d != i % 2:
                    continue
                part = aux.at[origins[d]] if i == 2 else buf.at[rows(origins[d] * Q_PART, Q_PART), :]
                moves.append(remote(
                    part, part, z_send.at[i, d, step - 1], z_recv.at[i, d, step - 1], z_ways[d]
                ))
        return moves

    def hop_y():
        moves = []
        for i, (buf, origin) in enumerate([(k, (y - 1 + NY) % NY), (v, (y + 1) % NY)]):
            part = buf.at[rows(origin * K_PART, K_PART), :]
            moves.append(remote(part, part, y_send.at[i], y_recv.at[i], y_ways[i]))
        return moves

    def start(moves):
        for copy in moves:
            copy.start()
        return moves

    def arrive(moves):
        for copy in moves:
            copy.wait_recv()

    aux_hops = start(hop_z(1))
    for copy in weights:
        copy.start()

    lane = lax.broadcasted_iota(jnp.int32, (Q_PART, LANES), 1)
    row = lax.broadcasted_iota(jnp.int32, (Q_PART, LANES), 0)
    ones = jnp.ones((K_PART, LANES), BF)

    def prepare_q(place):
        part = z_at(place)
        at_rows = rows(part * Q_PART, Q_PART)
        queries = q[at_rows, :].astype(F32) * 0.125
        turned = pltpu.roll(queries, LANES // 2, 1)
        grads = g[at_rows, :].astype(F32)
        columns = jnp.concatenate([aux[part].astype(F32)] * PAIRS, axis=0)
        source = lane // 4 == row // Q_OWN
        for h in range(2):
            head = lane // 64 == h
            qm[h, at_rows, :] = jnp.where(head, queries, 0.0).astype(BF)
            qr[h, at_rows, :] = jnp.where(head, 0.0, turned).astype(BF)
            gm[h, at_rows, :] = jnp.where(head, grads, 0.0).astype(BF)
            for dst, first in [(an, 0), (ad, 2)]:
                keep = jnp.logical_and(source, lane % 4 == first + h)
                dst[h, at_rows, :] = jnp.where(keep, columns, 0.0).astype(BF)

    def prepare_k(place):
        at_rows = rows(y_at(place) * K_PART, K_PART)
        kt[:, at_rows] = (k[at_rows, :].astype(F32) * 0.125).T.astype(BF)

    def attend(items):
        made = []
        for h, qp, kp in items:
            at_q, at_k = rows(z_at(qp) * Q_PART, Q_PART), rows(y_at(kp) * K_PART, K_PART)
            keys = jnp.concatenate([k[at_k, :], ones], axis=1)
            values = jnp.concatenate([v[at_k, :], ones], axis=1)
            scores = dot(keys, jnp.concatenate([qm[h, at_q, :], an[h, at_q, :]], axis=1), NT)
            grads = dot(values, jnp.concatenate([gm[h, at_q, :], ad[h, at_q, :]], axis=1), NT)
            probs = jnp.exp(scores)
            made.append((h, qp, kp, at_q, at_k, probs.astype(BF), (probs * grads).astype(BF)))
        by_keys, by_queries = {}, {}
        for item in made:
            by_keys.setdefault((item[0], str(item[2])), []).append(item)
            by_queries.setdefault((item[0], str(item[1])), []).append(item)
        for group in by_keys.values():
            h, at_k = group[0][0], group[0][4]
            left = jnp.concatenate([part for item in group for part in item[5:7]], axis=1)
            right = jnp.concatenate(
                [part for item in group for part in (gm[h, item[3], :], qr[h, item[3], :])], axis=0
            )
            acc[h, at_k, :] += dot(left, right, NN)
        for group in by_queries.values():
            h, at_q = group[0][0], group[0][3]
            head = pl.ds(h * 64, 64)
            left = jnp.concatenate([kt[head, item[4]] for item in group], axis=1)
            right = jnp.concatenate([item[6] for item in group], axis=0)
            dqt[head, at_q] += dot(left, right, NN)

    def loop(count, body):
        def step(i, _):
            body(i)
            return 0

        lax.fori_loop(0, count, step, 0)

    def both(qp, kp):
        attend([(0, qp, kp), (1, qp, kp)])

    def give_q(h, place):
        at_rows = rows(z_at(place) * Q_PART, Q_PART)
        return remote(
            send_q.at[h, :, at_rows], got_q.at[h, place - 1],
            rq_send.at[h, place - 1], rq_recv.at[h, place - 1], to_z(z_at(place)),
        )

    def give_k(h, place):
        at_rows = rows(y_at(place) * K_PART, K_PART)
        return remote(
            send_kv.at[h, at_rows, :], got_kv.at[h, place - 1],
            rkv_send.at[h, place - 1], rkv_recv.at[h, place - 1], to_y(y_at(place)),
        )

    def finish_q(h, place):
        at_rows = rows(z_at(place) * Q_PART, Q_PART)
        send_q[h, :, at_rows] = dqt[pl.ds(h * 64, 64), at_rows].astype(BF)
        give_q(h, place).start()

    def finish_k(h, place):
        at_rows = rows(y_at(place) * K_PART, K_PART)
        send_kv[h, at_rows, :] = acc[h, at_rows, :].astype(BF)
        give_k(h, place).start()

    prepare_q(0)
    prepare_k(0)
    both(0, 0)
    arrive(first_z)
    arrive(aux_hops)
    hops_2 = start(hop_z(2))
    loop(2, lambda i: prepare_q(i + 1))
    loop(2, lambda i: both(i + 1, 0))
    arrive(first_y)
    across = start(hop_y())
    loop(2, lambda i: prepare_k(i + 1))
    loop(3, lambda i: both(i, 1))
    arrive(hops_2)
    hops_3 = start(hop_z(3))
    loop(3, lambda i: both(i, 2))
    loop(2, lambda i: prepare_q(i + 3))
    loop(3, lambda i: attend([(0, 3, i), (0, 4, i)]))
    arrive(across)
    prepare_k(3)
    loop(3, lambda i: both(i, 3))
    arrive(hops_3)
    hops_4 = start(hop_z(4))
    loop(2, lambda i: both(i + 3, 3))
    loop(2, lambda i: prepare_q(i + 5))
    arrive(hops_4)
    prepare_q(7)

    def last_of_0(i):
        place = 3 - i
        attend([(0, 5, place), (0, 6, place), (0, 7, place)])

        @pl.when(place > 0)
        def _():
            finish_k(0, place)

    loop(4, last_of_0)
    loop(7, lambda i: finish_q(0, 7 - i))
    attend([(1, 5, 3), (1, 6, 3), (1, 7, 3)])
    finish_k(1, 3)
    loop(2, lambda i: finish_q(1, 2 - i))
    attend([(1, i, 1) for i in range(3, 8)])
    finish_k(1, 1)

    def last_of_1(i):
        place = 7 - i
        attend([(1, place, 2), (1, place, 0)])
        finish_q(1, place)

    loop(5, last_of_1)
    finish_k(1, 2)

    back = []

    def give_back(i, src, dst):
        for dx, dc in OTHERS:
            j = dx * NC + dc
            to = (x + dx) % NX * NC + (c + dc) % NC
            back.append(remote(
                src(to), dst.at[:, mine], b_send.at[i, j], b_recv.at[i, j], side(dx, dc)
            ))
            back[-1].start()
        back.append(pltpu.make_async_copy(src(me), dst.at[:, mine], bown_sem.at[i]))
        back[-1].start()

    at_rows = rows(z * Q_PART, Q_PART)
    halves = []
    for h in range(2):
        total = dqt[pl.ds(h * 64, 64), at_rows]
        for place in range(1, NZ):
            give_q(h, place).wait_recv()
            total += got_q[h, place - 1].astype(F32)
        halves.append(total)
    sum_q[...] = jnp.concatenate(halves, axis=0).T.astype(BF)
    give_back(0, lambda to: sum_q.at[rows(to * Q_OWN, Q_OWN), :], full_q)
    at_rows = rows(y * K_PART, K_PART)
    halves = []
    for h in range(2):
        total = acc[h, at_rows, :]
        for place in range(1, NY):
            give_k(h, place).wait_recv()
            total += got_kv[h, place - 1].astype(F32)
        halves.append(total)
    lane = lax.broadcasted_iota(jnp.int32, (K_PART, LANES), 1)
    turned = [pltpu.roll(half, LANES // 2, 1) for half in halves]
    sum_kv[0] = jnp.where(lane < 64, turned[0], turned[1]).astype(BF)
    sum_kv[1] = jnp.where(lane < 64, halves[0], halves[1]).astype(BF)
    give_back(1, lambda to: sum_kv.at[0, rows(to * K_OWN, K_OWN), :], full_k)
    give_back(2, lambda to: sum_kv.at[1, rows(to * K_OWN, K_OWN), :], full_v)

    for copy in sent + first_z + first_y + aux_hops + hops_2 + hops_3 + hops_4 + across:
        copy.wait_send()
    for h in range(2):
        for place in range(1, NZ):
            give_q(h, place).wait_send()
        for place in range(1, NY):
            give_k(h, place).wait_send()
    for copy in weights:
        copy.wait()
    for copy in back[:PAIRS]:
        copy.wait()
    out_q[...] = dot(full_q[...], wq[...], NT).astype(BF)
    for copy in back[PAIRS:]:
        copy.wait()
    out_kv[...] = (dot(full_k[...], wk[...], NT) + dot(full_v[...], wv[...], NT)).astype(BF)


def local(query_saved, key_saved, value_saved, out_grad, log_norm, row_delta, wq, wk, wv):
    width = query_saved.shape[1]
    hbm, vmem = pl.BlockSpec(memory_space=pl.ANY), pl.BlockSpec(memory_space=pltpu.VMEM)
    dma = pltpu.SemaphoreType.DMA
    return pl.pallas_call(
        kernel,
        out_shape=(
            jax.ShapeDtypeStruct((Q_OWN, width), BF),
            jax.ShapeDtypeStruct((K_OWN, width), BF),
        ),
        in_specs=[hbm] * 4 + [vmem] * 2 + [hbm] * 3,
        out_specs=(vmem, vmem),
        scratch_shapes=[
            pltpu.VMEM((Q_ALL, LANES), BF), pltpu.VMEM((Q_ALL, LANES), BF),
            pltpu.VMEM((K_ALL, LANES), BF), pltpu.VMEM((K_ALL, LANES), BF),
            pltpu.VMEM((Q_OWN, width), BF), pltpu.VMEM((PAIRS, Q_OWN, LANES), BF),
            pltpu.VMEM((NZ, Q_OWN, LANES), BF),
            *[pltpu.VMEM((2, Q_ALL, LANES), BF)] * 5,
            pltpu.VMEM((LANES, K_ALL), BF), pltpu.VMEM((LANES, Q_ALL), F32),
            pltpu.VMEM((2, K_ALL, LANES), F32),
            pltpu.VMEM((2, 64, Q_ALL), BF), pltpu.VMEM((2, K_ALL, LANES), BF),
            pltpu.VMEM((2, NZ - 1, 64, Q_PART), BF), pltpu.VMEM((2, NY - 1, K_PART, LANES), BF),
            pltpu.VMEM((Q_PART, LANES), BF), pltpu.VMEM((2, K_PART, LANES), BF),
            pltpu.VMEM((Q_OWN, width), BF), pltpu.VMEM((K_OWN, width), BF),
            pltpu.VMEM((K_OWN, width), BF),
            *[pltpu.VMEM((width, width), BF)] * 3,
            dma((5, PAIRS)), dma((5, PAIRS)), dma((4,)), dma((3,)),
            dma((2, 2, NX)), dma((2, 2, NX)), dma((2, 2, NX)), dma((2, 2, NX)),
            dma((3, 2, NZ // 2)), dma((3, 2, NZ // 2)), dma((2,)), dma((2,)),
            dma((2, NZ - 1)), dma((2, NZ - 1)), dma((2, NY - 1)), dma((2, NY - 1)),
            dma((3, PAIRS)), dma((3, PAIRS)), dma((3,)),
        ],
        compiler_params=pltpu.CompilerParams(
            collective_id=0, has_side_effects=True, vmem_limit_bytes=60 * 2**20
        ),
        name="attention_backward",
    )(query_saved, key_saved, value_saved, out_grad, log_norm, row_delta, wq, wk, wv)


def solution(mesh):
    in_specs = (
        P(("pb", "ka"), None),
        P(("ka", "pb"), None),
        P(("ka", "pb"), None),
        P(("pb", "ka"), None),
        P(None, ("pb", "ka")),
        P(None, ("pb", "ka")),
        P(),
        P(),
        P(),
    )
    out_specs = (P(("pb", "ka"), None), P(("ka", "pb"), None))
    return jax.shard_map(local, mesh=mesh, in_specs=in_specs, out_specs=out_specs, check_vma=False)
```

```python
import jax
import jax.numpy as jnp
from jax import lax
from jax.experimental import pallas as pl
from jax.experimental.pallas import tpu as pltpu
from jax.sharding import PartitionSpec as P

NX, NY, NZ, NC = 4, 4, 8, 2
PAIRS = NX * NC
LANES = 128
Q_OWN, K_OWN = 32, 64
Q_PART, K_PART = Q_OWN * PAIRS, K_OWN * PAIRS
Q_ALL, K_ALL = Q_PART * NZ, K_PART * NY
BF, F32 = jnp.bfloat16, jnp.float32
NT = (((1,), (1,)), ((), ()))
NN = (((1,), (0,)), ((), ()))
TN = (((0,), (0,)), ((), ()))
MESH = pl.DeviceIdType.MESH
OTHERS = [(dx, dc) for dx in range(NX) for dc in range(NC) if dx or dc]


def dot(a, b, dims):
    return lax.dot_general(a, b, dims, preferred_element_type=F32)


def rows(start, size):
    return pl.ds(pl.multiple_of(start, size), size)


def kernel(
    q_hbm, k_hbm, v_hbm, g_hbm, norm_hbm, delta_hbm, wq_hbm, wk_hbm, wv_hbm,
    out_q, out_kv,
    q, g, k, v, norm, delta, aux_out, aux_in, aux,
    qa, qr, ga, gm, ks, vs, kt, dqt, acc,
    send_q, send_kv, got_q, got_kv, sum_q, sum_kv, full_q, full_kv,
    wq, wk, wv, tally,
    own_sem, w_sem, sent_sem, a_recv, z_recv, y_recv, rq_recv, rkv_recv, b_recv,
):
    pb, ka = lax.axis_index("pb"), lax.axis_index("ka")
    z, y, c = pb % NZ, (ka // NC) % NY, ka % NC
    x = (ka // (NC * NY)) * 2 + pb // NZ
    me = x * NC + c

    def at(x, y, z, c):
        return {"pb": (x % 2) * NZ + z, "ka": (x // 2) * (NY * NC) + y * NC + c}

    def side(dx, dc):
        return at((x + dx) % NX, y, z, (c + dc) % NC)

    def ring(here, place, size):
        return (here + (place + 1) // 2 * (place % 2 * 2 - 1) + size) % size

    def z_at(place):
        return ring(z, place, NZ)

    def y_at(place):
        return ring(y, place, NY)

    def to_z(z):
        return at(x, y, z, c)

    def to_y(y):
        return at(x, y, z, c)

    def remote(src, dst, send, recv, device):
        return pltpu.make_async_remote_copy(
            src_ref=src, dst_ref=dst, send_sem=send, recv_sem=recv,
            device_id=device, device_id_type=MESH,
        )

    def landed(sem, count):
        part = tally.at[pl.ds(0, count), :]
        pltpu.make_async_copy(part, part, sem).wait()

    peers = [side(dx, dc) for dx, dc in OTHERS]
    peers += [to_z(z_at(i)) for i in range(1, NZ)] + [to_y(y_at(i)) for i in range(1, NY)]
    barrier = pltpu.get_barrier_semaphore()
    for peer in peers:
        pl.semaphore_signal(barrier, inc=1, device_id=peer, device_id_type=MESH)

    my_q = rows(z * Q_PART + me * Q_OWN, Q_OWN)
    my_k = rows(y * K_PART + me * K_OWN, K_OWN)
    exchanged = [(q_hbm, q, my_q), (g_hbm, g, my_q), (k_hbm, k, my_k), (v_hbm, v, my_k)]
    mine = rows(me * LANES, LANES)
    own = [
        pltpu.make_async_copy(src.at[:, mine], dst.at[at_rows, :], own_sem.at[i])
        for i, (src, dst, at_rows) in enumerate(exchanged)
    ]
    own += [
        pltpu.make_async_copy(norm_hbm, norm, own_sem.at[4]),
        pltpu.make_async_copy(delta_hbm, delta, own_sem.at[5]),
    ]
    for copy in own:
        copy.start()
    row = lax.broadcasted_iota(jnp.int32, (NX * NC * 2, PAIRS * LANES), 0)
    lane = lax.broadcasted_iota(jnp.int32, (NX * NC * 2, PAIRS * LANES), 1)
    same_pair = lane // LANES == row // 2
    pick = lambda first: jnp.where(
        jnp.logical_and(same_pair, lane % LANES == 4 * me + first + row % 2), -1.0, 0.0
    ).astype(BF)
    for copy in own:
        copy.wait()
    aux_out[...] = (dot(norm[...], pick(0), TN) + dot(delta[...], pick(2), TN)).astype(BF)
    acc[...] = jnp.zeros_like(acc)
    dqt[...] = jnp.zeros_like(dqt)
    pl.semaphore_wait(barrier, len(peers))

    for dx in (0, 1, 3, 2):
        for dc in range(NC):
            if not (dx or dc):
                continue
            j = dx * NC + dc
            cols = rows(((x + dx) % NX * NC + (c + dc) % NC) * LANES, LANES)
            for src, dst, at_rows in exchanged:
                remote(src.at[:, cols], dst.at[at_rows, :], sent_sem.at[0], a_recv.at[dx], side(dx, dc)).start()
            remote(aux_out.at[:, cols], aux_in.at[j], sent_sem.at[0], a_recv.at[dx], side(dx, dc)).start()
    per_peer = 3 * Q_OWN + 2 * K_OWN
    weights = [
        pltpu.make_async_copy(src, dst, w_sem.at[i])
        for i, (src, dst) in enumerate([(wq_hbm, wq), (wk_hbm, wk), (wv_hbm, wv)])
    ]

    z_ways = [to_z(z_at(1)), to_z(z_at(2))]
    y_ways = [to_y(y_at(1)), to_y(y_at(2))]
    for dx in (0, 1, 3, 2):
        landed(a_recv.at[dx], per_peer * (NC if dx else NC - 1))
        from_x = (x - dx + NX) % NX
        at_q = rows(z * Q_PART + from_x * NC * Q_OWN, NC * Q_OWN)
        at_k = rows(y * K_PART + from_x * NC * K_OWN, NC * K_OWN)
        for buf in (k, v):
            for d in range(2):
                part = buf.at[at_k, :]
                remote(part, part, sent_sem.at[1], y_recv.at[0], y_ways[d]).start()
        for buf in (q, g):
            for d in range(2):
                part = buf.at[at_q, :]
                remote(part, part, sent_sem.at[0], z_recv.at[0], z_ways[d]).start()
    aux_sum = aux_out[:, mine].astype(F32)
    for dx, dc in OTHERS:
        aux_sum += aux_in[dx * NC + dc].astype(F32)
    aux[z] = aux_sum.astype(BF)

    def hop_z(step):
        moves = []
        origins = [(z - step + 1 + NZ) % NZ, (z + step - 1) % NZ]
        for i, buf in enumerate([q, g, aux]):
            if step == 1 and i < 2:
                continue
            for d in range(2):
                if step == NZ // 2 and d != i % 2:
                    continue
                part = aux.at[origins[d]] if i == 2 else buf.at[rows(origins[d] * Q_PART, Q_PART), :]
                moves.append(remote(
                    part, part, sent_sem.at[0], z_recv.at[step - 1], z_ways[d]
                ))
        return moves

    def hop_y():
        moves = []
        for i, (buf, origin) in enumerate([(k, (y - 1 + NY) % NY), (v, (y + 1) % NY)]):
            part = buf.at[rows(origin * K_PART, K_PART), :]
            moves.append(remote(part, part, sent_sem.at[1], y_recv.at[1], y_ways[i]))
        return moves

    def start(moves):
        for copy in moves:
            copy.start()

    start(hop_z(1))
    for copy in weights:
        copy.start()

    lane = lax.broadcasted_iota(jnp.int32, (Q_PART, LANES), 1)
    row = lax.broadcasted_iota(jnp.int32, (Q_PART, LANES), 0)
    lane_k = lax.broadcasted_iota(jnp.int32, (K_PART, LANES), 1)

    def prepare_q(place):
        part = z_at(place)
        at_rows = rows(part * Q_PART, Q_PART)
        queries = q[at_rows, :].astype(F32) * 0.125
        turned = pltpu.roll(queries, LANES // 2, 1)
        grads = g[at_rows, :].astype(F32)
        extra = aux[part].astype(F32)
        for h in range(2):
            head = lane // 64 == h
            columns = jnp.concatenate([extra if h else pltpu.roll(extra, 64, 1)] * PAIRS, axis=0)
            source = (lane % 64) // 4 == row // Q_OWN
            less_norm = jnp.where(jnp.logical_and(source, lane % 4 == h), columns, 0.0)
            less_delta = jnp.where(jnp.logical_and(source, lane % 4 == 2 + h), columns, 0.0)
            qa[h, at_rows, :] = jnp.where(head, queries, less_norm).astype(BF)
            ga[h, at_rows, :] = jnp.where(head, grads, less_delta).astype(BF)
            gm[h, at_rows, :] = jnp.where(head, grads, 0.0).astype(BF)
            qr[h, at_rows, :] = jnp.where(head, 0.0, turned).astype(BF)

    def prepare_k(place):
        at_rows = rows(y_at(place) * K_PART, K_PART)
        keys = k[at_rows, :].astype(F32)
        values = v[at_rows, :].astype(F32)
        kt[:, at_rows] = (keys * 0.125).T.astype(BF)
        for h in range(2):
            ks[h, at_rows, :] = jnp.where(lane_k // 64 == h, keys, 1.0).astype(BF)
            vs[h, at_rows, :] = jnp.where(lane_k // 64 == h, values, 1.0).astype(BF)

    def attend(items):
        made = []
        for h, qp, kp in items:
            at_q, at_k = rows(z_at(qp) * Q_PART, Q_PART), rows(y_at(kp) * K_PART, K_PART)
            scores = dot(ks[h, at_k, :], qa[h, at_q, :], NT)
            grads = dot(vs[h, at_k, :], ga[h, at_q, :], NT)
            probs = jnp.exp(scores)
            made.append((h, qp, kp, at_q, at_k, probs.astype(BF), (probs * grads).astype(BF)))
        by_keys, by_queries = {}, {}
        for item in made:
            by_keys.setdefault((item[0], str(item[2])), []).append(item)
            by_queries.setdefault((item[0], str(item[1])), []).append(item)
        for group in by_keys.values():
            h, at_k = group[0][0], group[0][4]
            left = jnp.concatenate([part for item in group for part in item[5:7]], axis=1)
            right = jnp.concatenate(
                [part for item in group for part in (gm[h, item[3], :], qr[h, item[3], :])], axis=0
            )
            acc[h, at_k, :] += dot(left, right, NN)
        for group in by_queries.values():
            h, at_q = group[0][0], group[0][3]
            head = pl.ds(h * 64, 64)
            left = jnp.concatenate([kt[head, item[4]] for item in group], axis=1)
            right = jnp.concatenate([item[6] for item in group], axis=0)
            dqt[head, at_q] += dot(left, right, NN)

    def loop(count, body):
        def step(i, _):
            body(i)
            return 0

        lax.fori_loop(0, count, step, 0)

    def both(qp, kp):
        attend([(0, qp, kp), (1, qp, kp)])

    def give_q(h, place):
        at_rows = rows(z_at(place) * Q_PART, Q_PART)
        return remote(
            send_q.at[h, :, at_rows], got_q.at[h, place - 1],
            sent_sem.at[2], rq_recv.at[h], to_z(z_at(place)),
        )

    def give_k(h, place):
        at_rows = rows(y_at(place) * K_PART, K_PART)
        return remote(
            send_kv.at[h, at_rows, :], got_kv.at[h, place - 1],
            sent_sem.at[2], rkv_recv.at[h], to_y(y_at(place)),
        )

    def finish_q(h, place):
        at_rows = rows(z_at(place) * Q_PART, Q_PART)
        send_q[h, :, at_rows] = dqt[pl.ds(h * 64, 64), at_rows].astype(BF)
        give_q(h, place).start()

    def finish_k(h, place):
        at_rows = rows(y_at(place) * K_PART, K_PART)
        send_kv[h, at_rows, :] = acc[h, at_rows, :].astype(BF)
        give_k(h, place).start()

    hop_rows = 2 * (2 * Q_PART + Q_OWN)
    prepare_q(0)
    prepare_k(0)
    both(0, 0)
    landed(z_recv.at[0], hop_rows)
    start(hop_z(2))
    loop(2, lambda i: prepare_q(i + 1))
    loop(2, lambda i: both(i + 1, 0))
    landed(y_recv.at[0], 4 * K_PART)
    start(hop_y())
    loop(2, lambda i: prepare_k(i + 1))
    loop(3, lambda i: both(i, 1))
    landed(z_recv.at[1], hop_rows)
    start(hop_z(3))
    loop(3, lambda i: both(i, 2))
    loop(2, lambda i: prepare_q(i + 3))
    loop(3, lambda i: attend([(0, 3, i), (0, 4, i)]))
    landed(y_recv.at[1], 2 * K_PART)
    prepare_k(3)
    loop(3, lambda i: both(i, 3))
    landed(z_recv.at[2], hop_rows)
    start(hop_z(4))
    loop(2, lambda i: both(i + 3, 3))
    loop(2, lambda i: prepare_q(i + 5))
    landed(z_recv.at[3], 2 * Q_PART + Q_OWN)
    prepare_q(7)

    def last_of_0(i):
        place = 3 - i
        attend([(0, 5, place), (0, 6, place), (0, 7, place)])

        @pl.when(place > 0)
        def _():
            finish_k(0, place)

    loop(4, last_of_0)
    loop(7, lambda i: finish_q(0, 7 - i))
    attend([(1, 5, 3), (1, 6, 3), (1, 7, 3)])
    finish_k(1, 3)
    loop(2, lambda i: finish_q(1, 2 - i))
    attend([(1, i, 1) for i in range(3, 8)])
    finish_k(1, 1)

    def last_of_1(i):
        place = 7 - i
        attend([(1, place, 2), (1, place, 0)])
        finish_q(1, place)

    loop(3, last_of_1)
    attend([(1, 4, 2), (1, 3, 2)])
    finish_k(1, 2)

    def give_back(i, src, dst):
        for dx, dc in OTHERS:
            to = (x + dx) % NX * NC + (c + dc) % NC
            remote(src(to), dst.at[:, mine], sent_sem.at[3], b_recv.at[i], side(dx, dc)).start()
        copy = pltpu.make_async_copy(src(me), dst.at[:, mine], own_sem.at[i])
        copy.start()
        return copy

    own_q, own_k = rows(z * Q_PART, Q_PART), rows(y * K_PART, K_PART)

    def total_q(h):
        landed(rq_recv.at[h], (NZ - 1) * Q_PART // 2)
        total = dqt[pl.ds(h * 64, 64), own_q]
        for i in range(NZ - 1):
            total += got_q[h, i].astype(F32)
        return total

    def back_k(h):
        landed(rkv_recv.at[h], (NY - 1) * K_PART)
        total = acc[h, own_k, :]
        for i in range(NY - 1):
            total += got_kv[h, i].astype(F32)
        sum_kv[h] = total.astype(BF)
        return give_back(1 + h, lambda to: sum_kv.at[h, rows(to * K_OWN, K_OWN), :], full_kv.at[h])

    back_0 = back_k(0)
    dqt[pl.ds(0, 64), own_q] = total_q(0)
    attend([(1, 4, 0), (1, 3, 0)])
    finish_q(1, 4)
    finish_q(1, 3)
    sum_q[...] = jnp.concatenate([dqt[pl.ds(0, 64), own_q], total_q(1)], axis=0).T.astype(BF)
    back_q = give_back(0, lambda to: sum_q.at[rows(to * Q_OWN, Q_OWN), :], full_q)
    back_1 = back_k(1)

    z_rows = 2 * (NZ - 1) * Q_PART + (NZ - 1) * Q_OWN
    landed(sent_sem.at[0], (PAIRS - 1) * per_peer + z_rows)
    landed(sent_sem.at[1], 2 * (NY - 1) * K_PART)
    landed(sent_sem.at[2], (NZ - 1) * Q_PART + 2 * (NY - 1) * K_PART)
    landed(sent_sem.at[3], (PAIRS - 1) * (Q_OWN + 2 * K_OWN))
    for copy in weights:
        copy.wait()
    back_q.wait()
    landed(b_recv.at[0], (PAIRS - 1) * Q_OWN)
    out_q[...] = dot(full_q[...], wq[...], NT).astype(BF)
    for h, copy in enumerate([back_0, back_1]):
        copy.wait()
        landed(b_recv.at[1 + h], (PAIRS - 1) * K_OWN)
    low = lax.broadcasted_iota(jnp.int32, full_kv.shape[1:], 1) % LANES < 64
    first, second = full_kv[0].astype(F32), full_kv[1].astype(F32)
    width = first.shape[1]
    grad_k = jnp.where(low, pltpu.roll(first, width - 64, 1), pltpu.roll(second, 64, 1)).astype(BF)
    grad_v = jnp.where(low, first, second).astype(BF)
    out_kv[...] = (dot(grad_k, wk[...], NT) + dot(grad_v, wv[...], NT)).astype(BF)


def local(query_saved, key_saved, value_saved, out_grad, log_norm, row_delta, wq, wk, wv):
    width = query_saved.shape[1]
    hbm, vmem = pl.BlockSpec(memory_space=pl.ANY), pl.BlockSpec(memory_space=pltpu.VMEM)
    dma = pltpu.SemaphoreType.DMA
    return pl.pallas_call(
        kernel,
        out_shape=(
            jax.ShapeDtypeStruct((Q_OWN, width), BF),
            jax.ShapeDtypeStruct((K_OWN, width), BF),
        ),
        in_specs=[hbm] * 9,
        out_specs=(vmem, vmem),
        scratch_shapes=[
            pltpu.VMEM((Q_ALL, LANES), BF), pltpu.VMEM((Q_ALL, LANES), BF),
            pltpu.VMEM((K_ALL, LANES), BF), pltpu.VMEM((K_ALL, LANES), BF),
            pltpu.VMEM(log_norm.shape, BF), pltpu.VMEM(row_delta.shape, BF),
            pltpu.VMEM((Q_OWN, width), BF), pltpu.VMEM((PAIRS, Q_OWN, LANES), BF),
            pltpu.VMEM((NZ, Q_OWN, LANES), BF),
            *[pltpu.VMEM((2, Q_ALL, LANES), BF)] * 4, *[pltpu.VMEM((2, K_ALL, LANES), BF)] * 2,
            pltpu.VMEM((LANES, K_ALL), BF), pltpu.VMEM((LANES, Q_ALL), F32),
            pltpu.VMEM((2, K_ALL, LANES), F32),
            pltpu.VMEM((2, 64, Q_ALL), BF), pltpu.VMEM((2, K_ALL, LANES), BF),
            pltpu.VMEM((2, NZ - 1, 64, Q_PART), BF), pltpu.VMEM((2, NY - 1, K_PART, LANES), BF),
            pltpu.VMEM((Q_PART, LANES), BF), pltpu.VMEM((2, K_PART, LANES), BF),
            pltpu.VMEM((Q_OWN, width), BF), pltpu.VMEM((2, K_OWN, width), BF),
            *[pltpu.VMEM((width, width), BF)] * 3,
            pltpu.VMEM((8192, LANES), BF),
            dma((6,)), dma((3,)), dma((4,)), dma((NX,)), dma((NZ // 2,)), dma((2,)),
            dma((2,)), dma((2,)), dma((3,)),
        ],
        compiler_params=pltpu.CompilerParams(
            collective_id=0, has_side_effects=True, vmem_limit_bytes=60 * 2**20
        ),
        name="attention_backward",
    )(query_saved, key_saved, value_saved, out_grad, log_norm, row_delta, wq, wk, wv)


def solution(mesh):
    in_specs = (
        P(("pb", "ka"), None),
        P(("ka", "pb"), None),
        P(("ka", "pb"), None),
        P(("pb", "ka"), None),
        P(None, ("pb", "ka")),
        P(None, ("pb", "ka")),
        P(),
        P(),
        P(),
    )
    out_specs = (P(("pb", "ka"), None), P(("ka", "pb"), None))
    return jax.shard_map(local, mesh=mesh, in_specs=in_specs, out_specs=out_specs, check_vma=False)
```

```python
import jax
import jax.numpy as jnp
from jax import lax
from jax.experimental import pallas as pl
from jax.experimental.pallas import tpu as pltpu
from jax.sharding import PartitionSpec as P

NX, NY, NZ, NC = 4, 4, 8, 2
PAIRS = NX * NC
LANES = 128
Q_OWN, K_OWN = 32, 64
Q_PART, K_PART = Q_OWN * PAIRS, K_OWN * PAIRS
Q_ALL, K_ALL = Q_PART * NZ, K_PART * NY
BF, F32 = jnp.bfloat16, jnp.float32
NT = (((1,), (1,)), ((), ()))
NN = (((1,), (0,)), ((), ()))
TN = (((0,), (0,)), ((), ()))
MESH = pl.DeviceIdType.MESH
OTHERS = [(dx, dc) for dx in range(NX) for dc in range(NC) if dx or dc]


def dot(a, b, dims):
    return lax.dot_general(a, b, dims, preferred_element_type=F32)


def rows(start, size):
    return pl.ds(pl.multiple_of(start, size), size)


def kernel(
    q_hbm, k_hbm, v_hbm, g_hbm, norm_hbm, delta_hbm,
    full_q, full_kv,
    q, g, k, v, norm, delta, aux_out, aux_in, aux,
    qa, qr, ga, gm, ks, vs, kt, dqt, acc,
    send_q, send_kv, got_q, got_kv, sum_q, sum_kv, tally,
    own_sem, sent_sem, a_recv, z_recv, y_recv, rq_recv, rkv_recv, b_recv,
):
    pb, ka = lax.axis_index("pb"), lax.axis_index("ka")
    z, y, c = pb % NZ, (ka // NC) % NY, ka % NC
    x = (ka // (NC * NY)) * 2 + pb // NZ
    me = x * NC + c

    def at(x, y, z, c):
        return {"pb": (x % 2) * NZ + z, "ka": (x // 2) * (NY * NC) + y * NC + c}

    def side(dx, dc):
        return at((x + dx) % NX, y, z, (c + dc) % NC)

    def ring(here, place, size):
        return (here + (place + 1) // 2 * (place % 2 * 2 - 1) + size) % size

    def z_at(place):
        return ring(z, place, NZ)

    def y_at(place):
        return ring(y, place, NY)

    def to_z(z):
        return at(x, y, z, c)

    def to_y(y):
        return at(x, y, z, c)

    def remote(src, dst, send, recv, device):
        return pltpu.make_async_remote_copy(
            src_ref=src, dst_ref=dst, send_sem=send, recv_sem=recv,
            device_id=device, device_id_type=MESH,
        )

    def landed(sem, count):
        part = tally.at[pl.ds(0, count), :]
        pltpu.make_async_copy(part, part, sem).wait()

    peers = [side(dx, dc) for dx, dc in OTHERS]
    peers += [to_z(z_at(i)) for i in range(1, NZ)] + [to_y(y_at(i)) for i in range(1, NY)]
    barrier = pltpu.get_barrier_semaphore()
    for peer in peers:
        pl.semaphore_signal(barrier, inc=1, device_id=peer, device_id_type=MESH)

    my_q = rows(z * Q_PART + me * Q_OWN, Q_OWN)
    my_k = rows(y * K_PART + me * K_OWN, K_OWN)
    exchanged = [(q_hbm, q, my_q), (g_hbm, g, my_q), (k_hbm, k, my_k), (v_hbm, v, my_k)]
    mine = rows(me * LANES, LANES)
    own = [
        pltpu.make_async_copy(src.at[:, mine], dst.at[at_rows, :], own_sem.at[i])
        for i, (src, dst, at_rows) in enumerate(exchanged)
    ]
    own += [
        pltpu.make_async_copy(norm_hbm, norm, own_sem.at[4]),
        pltpu.make_async_copy(delta_hbm, delta, own_sem.at[5]),
    ]
    for copy in own:
        copy.start()
    row = lax.broadcasted_iota(jnp.int32, (NX * NC * 2, PAIRS * LANES), 0)
    lane = lax.broadcasted_iota(jnp.int32, (NX * NC * 2, PAIRS * LANES), 1)
    same_pair = lane // LANES == row // 2
    pick = lambda first: jnp.where(
        jnp.logical_and(same_pair, lane % LANES == 4 * me + first + row % 2), -1.0, 0.0
    ).astype(BF)
    for copy in own:
        copy.wait()
    aux_out[...] = (dot(norm[...], pick(0), TN) + dot(delta[...], pick(2), TN)).astype(BF)
    acc[...] = jnp.zeros_like(acc)
    dqt[...] = jnp.zeros_like(dqt)
    pl.semaphore_wait(barrier, len(peers))

    for dx in (0, 1, 3, 2):
        for dc in range(NC):
            if not (dx or dc):
                continue
            j = dx * NC + dc
            cols = rows(((x + dx) % NX * NC + (c + dc) % NC) * LANES, LANES)
            for src, dst, at_rows in exchanged:
                remote(src.at[:, cols], dst.at[at_rows, :], sent_sem.at[0], a_recv.at[dx], side(dx, dc)).start()
            remote(aux_out.at[:, cols], aux_in.at[j], sent_sem.at[0], a_recv.at[dx], side(dx, dc)).start()
    per_peer = 3 * Q_OWN + 2 * K_OWN

    z_ways = [to_z(z_at(1)), to_z(z_at(2))]
    y_ways = [to_y(y_at(1)), to_y(y_at(2))]
    for dx in (0, 1, 3, 2):
        landed(a_recv.at[dx], per_peer * (NC if dx else NC - 1))
        from_x = (x - dx + NX) % NX
        at_q = rows(z * Q_PART + from_x * NC * Q_OWN, NC * Q_OWN)
        at_k = rows(y * K_PART + from_x * NC * K_OWN, NC * K_OWN)
        for buf in (k, v):
            for d in range(2):
                part = buf.at[at_k, :]
                remote(part, part, sent_sem.at[1], y_recv.at[0], y_ways[d]).start()
        for buf in (q, g):
            for d in range(2):
                part = buf.at[at_q, :]
                remote(part, part, sent_sem.at[0], z_recv.at[0], z_ways[d]).start()
    aux_sum = aux_out[:, mine].astype(F32)
    for dx, dc in OTHERS:
        aux_sum += aux_in[dx * NC + dc].astype(F32)
    aux[z] = aux_sum.astype(BF)

    def hop_z(step):
        moves = []
        origins = [(z - step + 1 + NZ) % NZ, (z + step - 1) % NZ]
        for i, buf in enumerate([q, g, aux]):
            if step == 1 and i < 2:
                continue
            for d in range(2):
                if step == NZ // 2 and d != i % 2:
                    continue
                part = aux.at[origins[d]] if i == 2 else buf.at[rows(origins[d] * Q_PART, Q_PART), :]
                moves.append(remote(
                    part, part, sent_sem.at[0], z_recv.at[step - 1], z_ways[d]
                ))
        return moves

    def hop_y():
        moves = []
        for i, (buf, origin) in enumerate([(k, (y - 1 + NY) % NY), (v, (y + 1) % NY)]):
            part = buf.at[rows(origin * K_PART, K_PART), :]
            moves.append(remote(part, part, sent_sem.at[1], y_recv.at[1], y_ways[i]))
        return moves

    def start(moves):
        for copy in moves:
            copy.start()

    start(hop_z(1))

    lane = lax.broadcasted_iota(jnp.int32, (Q_PART, LANES), 1)
    row = lax.broadcasted_iota(jnp.int32, (Q_PART, LANES), 0)
    lane_k = lax.broadcasted_iota(jnp.int32, (K_PART, LANES), 1)

    def prepare_q(place):
        part = z_at(place)
        at_rows = rows(part * Q_PART, Q_PART)
        queries = q[at_rows, :].astype(F32) * 0.125
        turned = pltpu.roll(queries, LANES // 2, 1)
        grads = g[at_rows, :].astype(F32)
        extra = aux[part].astype(F32)
        for h in range(2):
            head = lane // 64 == h
            columns = jnp.concatenate([extra if h else pltpu.roll(extra, 64, 1)] * PAIRS, axis=0)
            source = (lane % 64) // 4 == row // Q_OWN
            less_norm = jnp.where(jnp.logical_and(source, lane % 4 == h), columns, 0.0)
            less_delta = jnp.where(jnp.logical_and(source, lane % 4 == 2 + h), columns, 0.0)
            qa[h, at_rows, :] = jnp.where(head, queries, less_norm).astype(BF)
            ga[h, at_rows, :] = jnp.where(head, grads, less_delta).astype(BF)
            gm[h, at_rows, :] = jnp.where(head, grads, 0.0).astype(BF)
            qr[h, at_rows, :] = jnp.where(head, 0.0, turned).astype(BF)

    def prepare_k(place):
        at_rows = rows(y_at(place) * K_PART, K_PART)
        keys = k[at_rows, :].astype(F32)
        values = v[at_rows, :].astype(F32)
        kt[:, at_rows] = (keys * 0.125).T.astype(BF)
        for h in range(2):
            ks[h, at_rows, :] = jnp.where(lane_k // 64 == h, keys, 1.0).astype(BF)
            vs[h, at_rows, :] = jnp.where(lane_k // 64 == h, values, 1.0).astype(BF)

    def attend(items):
        made = []
        for h, qp, kp in items:
            at_q, at_k = rows(z_at(qp) * Q_PART, Q_PART), rows(y_at(kp) * K_PART, K_PART)
            scores = dot(ks[h, at_k, :], qa[h, at_q, :], NT)
            grads = dot(vs[h, at_k, :], ga[h, at_q, :], NT)
            probs = jnp.exp(scores)
            made.append((h, qp, kp, at_q, at_k, probs.astype(BF), (probs * grads).astype(BF)))
        by_keys, by_queries = {}, {}
        for item in made:
            by_keys.setdefault((item[0], str(item[2])), []).append(item)
            by_queries.setdefault((item[0], str(item[1])), []).append(item)
        for group in by_keys.values():
            h, at_k = group[0][0], group[0][4]
            left = jnp.concatenate([part for item in group for part in item[5:7]], axis=1)
            right = jnp.concatenate(
                [part for item in group for part in (gm[h, item[3], :], qr[h, item[3], :])], axis=0
            )
            acc[h, at_k, :] += dot(left, right, NN)
        for group in by_queries.values():
            h, at_q = group[0][0], group[0][3]
            head = pl.ds(h * 64, 64)
            left = jnp.concatenate([kt[head, item[4]] for item in group], axis=1)
            right = jnp.concatenate([item[6] for item in group], axis=0)
            dqt[head, at_q] += dot(left, right, NN)

    def loop(count, body):
        def step(i, _):
            body(i)
            return 0

        lax.fori_loop(0, count, step, 0)

    def both(qps, kp):
        attend([(h, qp, kp) for h in range(2) for qp in qps])

    def give_q(h, place):
        at_rows = rows(z_at(place) * Q_PART, Q_PART)
        return remote(
            send_q.at[h, :, at_rows], got_q.at[h, place - 1],
            sent_sem.at[2], rq_recv.at[h], to_z(z_at(place)),
        )

    def give_k(h, place):
        at_rows = rows(y_at(place) * K_PART, K_PART)
        return remote(
            send_kv.at[h, at_rows, :], got_kv.at[h, place - 1],
            sent_sem.at[2], rkv_recv.at[h], to_y(y_at(place)),
        )

    def finish_q(h, place):
        at_rows = rows(z_at(place) * Q_PART, Q_PART)
        send_q[h, :, at_rows] = dqt[pl.ds(h * 64, 64), at_rows].astype(BF)
        give_q(h, place).start()

    def finish_k(h, place):
        at_rows = rows(y_at(place) * K_PART, K_PART)
        send_kv[h, at_rows, :] = acc[h, at_rows, :].astype(BF)
        give_k(h, place).start()

    hop_rows = 2 * (2 * Q_PART + Q_OWN)
    prepare_q(0)
    prepare_k(0)
    both([0], 0)
    landed(z_recv.at[0], hop_rows)
    start(hop_z(2))
    prepare_q(1)
    prepare_q(2)
    both([1, 2], 0)
    landed(y_recv.at[0], 4 * K_PART)
    start(hop_y())
    prepare_k(1)
    both([0, 1, 2], 1)
    prepare_k(2)
    landed(z_recv.at[1], hop_rows)
    start(hop_z(3))
    both([0, 1, 2], 2)
    prepare_q(3)
    prepare_q(4)
    attend([(0, qp, kp) for kp in range(3) for qp in (3, 4)])
    landed(y_recv.at[1], 2 * K_PART)
    prepare_k(3)
    both([0, 1, 2], 3)
    landed(z_recv.at[2], hop_rows)
    start(hop_z(4))
    both([3, 4], 3)
    prepare_q(5)
    prepare_q(6)
    landed(z_recv.at[3], 2 * Q_PART + Q_OWN)
    prepare_q(7)

    def last_of_0(i):
        place = 3 - i
        attend([(0, 5, place), (0, 6, place), (0, 7, place)])

        @pl.when(place > 0)
        def _():
            finish_k(0, place)

    loop(4, last_of_0)
    loop(7, lambda i: finish_q(0, 7 - i))
    attend([(1, 5, 3), (1, 6, 3), (1, 7, 3)])
    finish_k(1, 3)
    loop(2, lambda i: finish_q(1, 2 - i))
    attend([(1, i, 1) for i in range(3, 8)])
    finish_k(1, 1)

    def last_of_1(i):
        place = 7 - i
        attend([(1, place, 2), (1, place, 0)])
        finish_q(1, place)

    loop(3, last_of_1)
    attend([(1, 4, 2), (1, 3, 2)])
    finish_k(1, 2)

    def give_back(i, src, dst):
        for dx, dc in OTHERS:
            to = (x + dx) % NX * NC + (c + dc) % NC
            remote(src(to), dst.at[:, mine], sent_sem.at[3], b_recv.at[i], side(dx, dc)).start()
        copy = pltpu.make_async_copy(src(me), dst.at[:, mine], own_sem.at[i])
        copy.start()
        return copy

    own_q, own_k = rows(z * Q_PART, Q_PART), rows(y * K_PART, K_PART)

    def total_q(h):
        landed(rq_recv.at[h], (NZ - 1) * Q_PART // 2)
        total = dqt[pl.ds(h * 64, 64), own_q]
        for i in range(NZ - 1):
            total += got_q[h, i].astype(F32)
        return total

    def back_k(h):
        landed(rkv_recv.at[h], (NY - 1) * K_PART)
        total = acc[h, own_k, :]
        for i in range(NY - 1):
            total += got_kv[h, i].astype(F32)
        sum_kv[h] = total.astype(BF)
        return give_back(1 + h, lambda to: sum_kv.at[h, rows(to * K_OWN, K_OWN), :], full_kv.at[h])

    back_0 = back_k(0)
    dqt[pl.ds(0, 64), own_q] = total_q(0)
    attend([(1, 4, 0), (1, 3, 0)])
    finish_q(1, 4)
    finish_q(1, 3)
    sum_q[...] = jnp.concatenate([dqt[pl.ds(0, 64), own_q], total_q(1)], axis=0).T.astype(BF)
    back_q = give_back(0, lambda to: sum_q.at[rows(to * Q_OWN, Q_OWN), :], full_q)
    back_1 = back_k(1)

    z_rows = 2 * (NZ - 1) * Q_PART + (NZ - 1) * Q_OWN
    landed(sent_sem.at[0], (PAIRS - 1) * per_peer + z_rows)
    landed(sent_sem.at[1], 2 * (NY - 1) * K_PART)
    landed(sent_sem.at[2], (NZ - 1) * Q_PART + 2 * (NY - 1) * K_PART)
    landed(sent_sem.at[3], (PAIRS - 1) * (Q_OWN + 2 * K_OWN))
    back_q.wait()
    landed(b_recv.at[0], (PAIRS - 1) * Q_OWN)
    for h, copy in enumerate([back_0, back_1]):
        copy.wait()
        landed(b_recv.at[1 + h], (PAIRS - 1) * K_OWN)


def project(full_q, full_kv, wq, wk, wv, out_q, out_kv):
    out_q[...] = dot(full_q[...], wq[...], NT).astype(BF)
    low = lax.broadcasted_iota(jnp.int32, full_kv.shape[1:], 1) % LANES < 64
    first, second = full_kv[0].astype(F32), full_kv[1].astype(F32)
    width = first.shape[1]
    grad_k = jnp.where(low, pltpu.roll(first, width - 64, 1), pltpu.roll(second, 64, 1)).astype(BF)
    grad_v = jnp.where(low, first, second).astype(BF)
    out_kv[...] = (dot(grad_k, wk[...], NT) + dot(grad_v, wv[...], NT)).astype(BF)


def local(query_saved, key_saved, value_saved, out_grad, log_norm, row_delta, wq, wk, wv):
    width = query_saved.shape[1]
    hbm, vmem = pl.BlockSpec(memory_space=pltpu.HBM), pl.BlockSpec(memory_space=pltpu.VMEM)
    dma = pltpu.SemaphoreType.DMA
    full_q, full_kv = pl.pallas_call(
        kernel,
        out_shape=(
            jax.ShapeDtypeStruct((Q_OWN, width), BF),
            jax.ShapeDtypeStruct((2, K_OWN, width), BF),
        ),
        in_specs=[hbm] * 6,
        out_specs=(vmem, vmem),
        scratch_shapes=[
            pltpu.VMEM((Q_ALL, LANES), BF), pltpu.VMEM((Q_ALL, LANES), BF),
            pltpu.VMEM((K_ALL, LANES), BF), pltpu.VMEM((K_ALL, LANES), BF),
            pltpu.VMEM(log_norm.shape, BF), pltpu.VMEM(row_delta.shape, BF),
            pltpu.VMEM((Q_OWN, width), BF), pltpu.VMEM((PAIRS, Q_OWN, LANES), BF),
            pltpu.VMEM((NZ, Q_OWN, LANES), BF),
            *[pltpu.VMEM((2, Q_ALL, LANES), BF)] * 4, *[pltpu.VMEM((2, K_ALL, LANES), BF)] * 2,
            pltpu.VMEM((LANES, K_ALL), BF), pltpu.VMEM((LANES, Q_ALL), F32),
            pltpu.VMEM((2, K_ALL, LANES), F32),
            pltpu.VMEM((2, 64, Q_ALL), BF), pltpu.VMEM((2, K_ALL, LANES), BF),
            pltpu.VMEM((2, NZ - 1, 64, Q_PART), BF), pltpu.VMEM((2, NY - 1, K_PART, LANES), BF),
            pltpu.VMEM((Q_PART, LANES), BF), pltpu.VMEM((2, K_PART, LANES), BF),
            pltpu.VMEM((8192, LANES), BF),
            dma((6,)), dma((4,)), dma((NX,)), dma((NZ // 2,)), dma((2,)),
            dma((2,)), dma((2,)), dma((3,)),
        ],
        compiler_params=pltpu.CompilerParams(
            collective_id=0, has_side_effects=True, vmem_limit_bytes=40 * 2**20
        ),
        cost_estimate=pl.CostEstimate(
            flops=20 * Q_ALL * K_ALL * 64, bytes_accessed=2**20, transcendentals=2 * Q_ALL * K_ALL
        ),
        name="attention_backward",
    )(*[pltpu.with_memory_space_constraint(a, pltpu.HBM) for a in (query_saved, key_saved, value_saved, out_grad, log_norm, row_delta)])
    return pl.pallas_call(
        project,
        out_shape=(
            jax.ShapeDtypeStruct((Q_OWN, width), BF),
            jax.ShapeDtypeStruct((K_OWN, width), BF),
        ),
        in_specs=[vmem] * 5,
        out_specs=(vmem, vmem),
        compiler_params=pltpu.CompilerParams(vmem_limit_bytes=16 * 2**20),
        name="projections",
    )(full_q, full_kv, wq, wk, wv)


def solution(mesh):
    in_specs = (
        P(("pb", "ka"), None),
        P(("ka", "pb"), None),
        P(("ka", "pb"), None),
        P(("pb", "ka"), None),
        P(None, ("pb", "ka")),
        P(None, ("pb", "ka")),
        P(),
        P(),
        P(),
    )
    out_specs = (P(("pb", "ka"), None), P(("ka", "pb"), None))
    return jax.shard_map(local, mesh=mesh, in_specs=in_specs, out_specs=out_specs, check_vma=False)
```

```python
import jax
import jax.numpy as jnp
from jax import lax
from jax.experimental import pallas as pl
from jax.experimental.pallas import tpu as pltpu
from jax.sharding import PartitionSpec as P

NX, NY, NZ, NC = 4, 4, 8, 2
PAIRS = NX * NC
LANES = 128
Q_OWN, K_OWN = 32, 64
Q_PART, K_PART = Q_OWN * PAIRS, K_OWN * PAIRS
Q_ALL, K_ALL = Q_PART * NZ, K_PART * NY
BF, F32 = jnp.bfloat16, jnp.float32
NT = (((1,), (1,)), ((), ()))
NN = (((1,), (0,)), ((), ()))
TN = (((0,), (0,)), ((), ()))
MESH = pl.DeviceIdType.MESH
OTHERS = [(dx, dc) for dx in range(NX) for dc in range(NC) if dx or dc]


def dot(a, b, dims):
    return lax.dot_general(a, b, dims, preferred_element_type=F32)


def rows(start, size):
    return pl.ds(pl.multiple_of(start, size), size)


def kernel(
    q_hbm, k_hbm, v_hbm, g_hbm, norm_hbm, delta_hbm,
    full_q, full_kv,
    q, g, k, v, norm, delta, aux_out, aux_in, aux,
    qa, qr, ga, gm, ks, vs, kt, dqt, acc,
    send_q, send_kv, got_q, got_kv, sum_q, sum_kv, tally,
    own_sem, sent_sem, a_recv, ak_recv, z_recv, y_recv, rq_recv, rkv_recv, b_recv,
):
    pb, ka = lax.axis_index("pb"), lax.axis_index("ka")
    z, y, c = pb % NZ, (ka // NC) % NY, ka % NC
    x = (ka // (NC * NY)) * 2 + pb // NZ
    me = x * NC + c

    def at(x, y, z, c):
        return {"pb": (x % 2) * NZ + z, "ka": (x // 2) * (NY * NC) + y * NC + c}

    def side(dx, dc):
        return at((x + dx) % NX, y, z, (c + dc) % NC)

    def ring(here, place, size):
        return (here + (place + 1) // 2 * (place % 2 * 2 - 1) + size) % size

    def z_at(place):
        return ring(z, place, NZ)

    def y_at(place):
        return ring(y, place, NY)

    def to_z(z):
        return at(x, y, z, c)

    def to_y(y):
        return at(x, y, z, c)

    def remote(src, dst, send, recv, device):
        return pltpu.make_async_remote_copy(
            src_ref=src, dst_ref=dst, send_sem=send, recv_sem=recv,
            device_id=device, device_id_type=MESH,
        )

    def landed(sem, count):
        part = tally.at[pl.ds(0, count), :]
        pltpu.make_async_copy(part, part, sem).wait()

    peers = [side(dx, dc) for dx, dc in OTHERS]
    peers += [to_z(z_at(i)) for i in range(1, NZ)] + [to_y(y_at(i)) for i in range(1, NY)]
    barrier = pltpu.get_barrier_semaphore()
    for peer in peers:
        pl.semaphore_signal(barrier, inc=1, device_id=peer, device_id_type=MESH)

    my_q = rows(z * Q_PART + me * Q_OWN, Q_OWN)
    my_k = rows(y * K_PART + me * K_OWN, K_OWN)
    exchanged = [(q_hbm, q, my_q), (g_hbm, g, my_q), (k_hbm, k, my_k), (v_hbm, v, my_k)]
    mine = rows(me * LANES, LANES)
    own = [
        pltpu.make_async_copy(src.at[:, mine], dst.at[at_rows, :], own_sem.at[i])
        for i, (src, dst, at_rows) in enumerate(exchanged)
    ]
    own += [
        pltpu.make_async_copy(norm_hbm, norm, own_sem.at[4]),
        pltpu.make_async_copy(delta_hbm, delta, own_sem.at[5]),
    ]
    for copy in own:
        copy.start()
    row = lax.broadcasted_iota(jnp.int32, (NX * NC * 2, PAIRS * LANES), 0)
    lane = lax.broadcasted_iota(jnp.int32, (NX * NC * 2, PAIRS * LANES), 1)
    same_pair = lane // LANES == row // 2
    pick = lambda first: jnp.where(
        jnp.logical_and(same_pair, lane % LANES == 4 * me + first + row % 2), -1.0, 0.0
    ).astype(BF)
    for copy in own:
        copy.wait()
    aux_out[...] = (dot(norm[...], pick(0), TN) + dot(delta[...], pick(2), TN)).astype(BF)
    acc[...] = jnp.zeros_like(acc)
    dqt[...] = jnp.zeros_like(dqt)
    pl.semaphore_wait(barrier, len(peers))

    def exchange(arrays, arrived):
        for dx in (0, 1, 3, 2):
            for dc in range(NC):
                if not (dx or dc):
                    continue
                j = dx * NC + dc
                cols = rows(((x + dx) % NX * NC + (c + dc) % NC) * LANES, LANES)
                for src, dst, at_rows in arrays:
                    to = dst.at[j] if at_rows is None else dst.at[at_rows, :]
                    remote(src.at[:, cols], to, sent_sem.at[0], arrived.at[dx], side(dx, dc)).start()

    exchange(exchanged[:2] + [(aux_out, aux_in, None)], a_recv)
    exchange(exchanged[2:], ak_recv)
    per_peer = 3 * Q_OWN + 2 * K_OWN

    z_ways = [to_z(z_at(1)), to_z(z_at(2))]
    y_ways = [to_y(y_at(1)), to_y(y_at(2))]
    for dx in (0, 1, 3, 2):
        landed(a_recv.at[dx], 3 * Q_OWN * (NC if dx else NC - 1))
        from_x = (x - dx + NX) % NX
        at_q = rows(z * Q_PART + from_x * NC * Q_OWN, NC * Q_OWN)
        for buf in (q, g):
            for d in range(2):
                part = buf.at[at_q, :]
                remote(part, part, sent_sem.at[0], z_recv.at[0], z_ways[d]).start()

    def first_y(dx):
        landed(ak_recv.at[dx], 2 * K_OWN * (NC if dx else NC - 1))
        from_x = (x - dx + NX) % NX
        at_k = rows(y * K_PART + from_x * NC * K_OWN, NC * K_OWN)
        for buf in (k, v):
            for d in range(2):
                part = buf.at[at_k, :]
                remote(part, part, sent_sem.at[1], y_recv.at[0], y_ways[d]).start()

    first_y(0)
    aux_sum = aux_out[:, mine].astype(F32)
    for dx, dc in OTHERS:
        aux_sum += aux_in[dx * NC + dc].astype(F32)
    aux[z] = aux_sum.astype(BF)

    def hop_z(step):
        moves = []
        origins = [(z - step + 1 + NZ) % NZ, (z + step - 1) % NZ]
        for i, buf in enumerate([q, g, aux]):
            if step == 1 and i < 2:
                continue
            for d in range(2):
                if step == NZ // 2 and d != i % 2:
                    continue
                part = aux.at[origins[d]] if i == 2 else buf.at[rows(origins[d] * Q_PART, Q_PART), :]
                moves.append(remote(
                    part, part, sent_sem.at[0], z_recv.at[step - 1], z_ways[d]
                ))
        return moves

    def hop_y():
        moves = []
        for i, (buf, origin) in enumerate([(k, (y - 1 + NY) % NY), (v, (y + 1) % NY)]):
            part = buf.at[rows(origin * K_PART, K_PART), :]
            moves.append(remote(part, part, sent_sem.at[1], y_recv.at[1], y_ways[i]))
        return moves

    def start(moves):
        for copy in moves:
            copy.start()

    start(hop_z(1))
    for dx in (1, 3, 2):
        first_y(dx)

    lane = lax.broadcasted_iota(jnp.int32, (Q_PART, LANES), 1)
    row = lax.broadcasted_iota(jnp.int32, (Q_PART, LANES), 0)
    lane_k = lax.broadcasted_iota(jnp.int32, (K_PART, LANES), 1)

    def prepare_q(place):
        part = z_at(place)
        at_rows = rows(part * Q_PART, Q_PART)
        queries = q[at_rows, :].astype(F32) * 0.125
        turned = pltpu.roll(queries, LANES // 2, 1)
        grads = g[at_rows, :].astype(F32)
        extra = aux[part].astype(F32)
        for h in range(2):
            head = lane // 64 == h
            columns = jnp.concatenate([extra if h else pltpu.roll(extra, 64, 1)] * PAIRS, axis=0)
            source = (lane % 64) // 4 == row // Q_OWN
            less_norm = jnp.where(jnp.logical_and(source, lane % 4 == h), columns, 0.0)
            less_delta = jnp.where(jnp.logical_and(source, lane % 4 == 2 + h), columns, 0.0)
            qa[h, at_rows, :] = jnp.where(head, queries, less_norm).astype(BF)
            ga[h, at_rows, :] = jnp.where(head, grads, less_delta).astype(BF)
            gm[h, at_rows, :] = jnp.where(head, grads, 0.0).astype(BF)
            qr[h, at_rows, :] = jnp.where(head, 0.0, turned).astype(BF)

    def prepare_k(place):
        at_rows = rows(y_at(place) * K_PART, K_PART)
        keys = k[at_rows, :].astype(F32)
        values = v[at_rows, :].astype(F32)
        kt[:, at_rows] = (keys * 0.125).T.astype(BF)
        for h in range(2):
            ks[h, at_rows, :] = jnp.where(lane_k // 64 == h, keys, 1.0).astype(BF)
            vs[h, at_rows, :] = jnp.where(lane_k // 64 == h, values, 1.0).astype(BF)

    def attend(items):
        made = []
        for h, qp, kp in items:
            at_q, at_k = rows(z_at(qp) * Q_PART, Q_PART), rows(y_at(kp) * K_PART, K_PART)
            scores = dot(ks[h, at_k, :], qa[h, at_q, :], NT)
            grads = dot(vs[h, at_k, :], ga[h, at_q, :], NT)
            probs = jnp.exp(scores)
            made.append((h, qp, kp, at_q, at_k, probs.astype(BF), (probs * grads).astype(BF)))
        by_keys, by_queries = {}, {}
        for item in made:
            by_keys.setdefault((item[0], str(item[2])), []).append(item)
            by_queries.setdefault((item[0], str(item[1])), []).append(item)
        for group in by_keys.values():
            h, at_k = group[0][0], group[0][4]
            left = jnp.concatenate([part for item in group for part in item[5:7]], axis=1)
            right = jnp.concatenate(
                [part for item in group for part in (gm[h, item[3], :], qr[h, item[3], :])], axis=0
            )
            acc[h, at_k, :] += dot(left, right, NN)
        for group in by_queries.values():
            h, at_q = group[0][0], group[0][3]
            head = pl.ds(h * 64, 64)
            left = jnp.concatenate([kt[head, item[4]] for item in group], axis=1)
            right = jnp.concatenate([item[6] for item in group], axis=0)
            dqt[head, at_q] += dot(left, right, NN)

    def loop(count, body):
        def step(i, _):
            body(i)
            return 0

        lax.fori_loop(0, count, step, 0)

    def both(qps, kp):
        attend([(h, qp, kp) for h in range(2) for qp in qps])

    def give_q(h, place):
        at_rows = rows(z_at(place) * Q_PART, Q_PART)
        return remote(
            send_q.at[h, :, at_rows], got_q.at[h, place - 1],
            sent_sem.at[2], rq_recv.at[h], to_z(z_at(place)),
        )

    def give_k(h, place):
        at_rows = rows(y_at(place) * K_PART, K_PART)
        return remote(
            send_kv.at[h, at_rows, :], got_kv.at[h, place - 1],
            sent_sem.at[2], rkv_recv.at[h], to_y(y_at(place)),
        )

    def finish_q(h, place):
        at_rows = rows(z_at(place) * Q_PART, Q_PART)
        send_q[h, :, at_rows] = dqt[pl.ds(h * 64, 64), at_rows].astype(BF)
        give_q(h, place).start()

    def finish_k(h, place):
        at_rows = rows(y_at(place) * K_PART, K_PART)
        send_kv[h, at_rows, :] = acc[h, at_rows, :].astype(BF)
        give_k(h, place).start()

    hop_rows = 2 * (2 * Q_PART + Q_OWN)
    prepare_q(0)
    prepare_k(0)
    both([0], 0)
    landed(z_recv.at[0], hop_rows)
    start(hop_z(2))
    prepare_q(1)
    prepare_q(2)
    both([1, 2], 0)
    landed(z_recv.at[1], hop_rows)
    start(hop_z(3))
    prepare_q(3)
    prepare_q(4)
    both([3, 4], 0)
    landed(y_recv.at[0], 4 * K_PART)
    start(hop_y())
    prepare_k(1)
    both([0, 1, 2], 1)
    prepare_k(2)
    both([0, 1, 2], 2)
    landed(z_recv.at[2], hop_rows)
    start(hop_z(4))
    attend([(0, qp, kp) for kp in (1, 2) for qp in (3, 4)])
    landed(y_recv.at[1], 2 * K_PART)
    prepare_k(3)
    both([0, 1, 2], 3)
    both([3, 4], 3)
    prepare_q(5)
    prepare_q(6)
    landed(z_recv.at[3], 2 * Q_PART + Q_OWN)
    prepare_q(7)

    def last_of_0(i):
        place = 3 - i
        attend([(0, 5, place), (0, 6, place), (0, 7, place)])

        @pl.when(place > 0)
        def _():
            finish_k(0, place)

    loop(4, last_of_0)
    loop(7, lambda i: finish_q(0, 7 - i))
    attend([(1, 5, 3), (1, 6, 3), (1, 7, 3)])
    finish_k(1, 3)
    loop(2, lambda i: finish_q(1, 2 - i))
    attend([(1, i, 1) for i in range(3, 8)])
    finish_k(1, 1)

    attend([(1, qp, kp) for qp in (7, 6) for kp in (2, 0)])
    finish_q(1, 7)
    finish_q(1, 6)
    attend([(1, 5, 2), (1, 4, 2), (1, 3, 2)])
    finish_k(1, 2)
    finish_q(1, 4)
    finish_q(1, 3)

    def give_back(i, src, dst):
        for dx, dc in OTHERS:
            to = (x + dx) % NX * NC + (c + dc) % NC
            remote(src(to), dst.at[:, mine], sent_sem.at[3], b_recv.at[i], side(dx, dc)).start()
        copy = pltpu.make_async_copy(src(me), dst.at[:, mine], own_sem.at[i])
        copy.start()
        return copy

    own_q, own_k = rows(z * Q_PART, Q_PART), rows(y * K_PART, K_PART)

    def total_q(h):
        landed(rq_recv.at[h], (NZ - 1) * Q_PART // 2)
        total = dqt[pl.ds(h * 64, 64), own_q]
        for i in range(NZ - 1):
            total += got_q[h, i].astype(F32)
        return total

    def back_k(h):
        landed(rkv_recv.at[h], (NY - 1) * K_PART)
        total = acc[h, own_k, :]
        for i in range(NY - 1):
            total += got_kv[h, i].astype(F32)
        sum_kv[h] = total.astype(BF)
        return give_back(1 + h, lambda to: sum_kv.at[h, rows(to * K_OWN, K_OWN), :], full_kv.at[h])

    attend([(1, 5, 0)])
    finish_q(1, 5)
    back_0 = back_k(0)
    dqt[pl.ds(0, 64), own_q] = total_q(0)
    sum_q[...] = jnp.concatenate([dqt[pl.ds(0, 64), own_q], total_q(1)], axis=0).T.astype(BF)
    back_q = give_back(0, lambda to: sum_q.at[rows(to * Q_OWN, Q_OWN), :], full_q)
    back_1 = back_k(1)

    z_rows = 2 * (NZ - 1) * Q_PART + (NZ - 1) * Q_OWN
    landed(sent_sem.at[0], (PAIRS - 1) * per_peer + z_rows)
    landed(sent_sem.at[1], 2 * (NY - 1) * K_PART)
    landed(sent_sem.at[2], (NZ - 1) * Q_PART + 2 * (NY - 1) * K_PART)
    landed(sent_sem.at[3], (PAIRS - 1) * (Q_OWN + 2 * K_OWN))
    back_q.wait()
    landed(b_recv.at[0], (PAIRS - 1) * Q_OWN)
    for h, copy in enumerate([back_0, back_1]):
        copy.wait()
        landed(b_recv.at[1 + h], (PAIRS - 1) * K_OWN)


def project(full_q, full_kv, wq, wk, wv, out_q, out_kv):
    out_q[...] = dot(full_q[...], wq[...], NT).astype(BF)
    low = lax.broadcasted_iota(jnp.int32, full_kv.shape[1:], 1) % LANES < 64
    first, second = full_kv[0].astype(F32), full_kv[1].astype(F32)
    width = first.shape[1]
    grad_k = jnp.where(low, pltpu.roll(first, width - 64, 1), pltpu.roll(second, 64, 1)).astype(BF)
    grad_v = jnp.where(low, first, second).astype(BF)
    out_kv[...] = (dot(grad_k, wk[...], NT) + dot(grad_v, wv[...], NT)).astype(BF)


def local(query_saved, key_saved, value_saved, out_grad, log_norm, row_delta, wq, wk, wv):
    width = query_saved.shape[1]
    hbm, vmem = pl.BlockSpec(memory_space=pltpu.HBM), pl.BlockSpec(memory_space=pltpu.VMEM)
    dma = pltpu.SemaphoreType.DMA
    full_q, full_kv = pl.pallas_call(
        kernel,
        out_shape=(
            jax.ShapeDtypeStruct((Q_OWN, width), BF),
            jax.ShapeDtypeStruct((2, K_OWN, width), BF),
        ),
        in_specs=[hbm] * 6,
        out_specs=(vmem, vmem),
        scratch_shapes=[
            pltpu.VMEM((Q_ALL, LANES), BF), pltpu.VMEM((Q_ALL, LANES), BF),
            pltpu.VMEM((K_ALL, LANES), BF), pltpu.VMEM((K_ALL, LANES), BF),
            pltpu.VMEM(log_norm.shape, BF), pltpu.VMEM(row_delta.shape, BF),
            pltpu.VMEM((Q_OWN, width), BF), pltpu.VMEM((PAIRS, Q_OWN, LANES), BF),
            pltpu.VMEM((NZ, Q_OWN, LANES), BF),
            *[pltpu.VMEM((2, Q_ALL, LANES), BF)] * 4, *[pltpu.VMEM((2, K_ALL, LANES), BF)] * 2,
            pltpu.VMEM((LANES, K_ALL), BF), pltpu.VMEM((LANES, Q_ALL), F32),
            pltpu.VMEM((2, K_ALL, LANES), F32),
            pltpu.VMEM((2, 64, Q_ALL), BF), pltpu.VMEM((2, K_ALL, LANES), BF),
            pltpu.VMEM((2, NZ - 1, 64, Q_PART), BF), pltpu.VMEM((2, NY - 1, K_PART, LANES), BF),
            pltpu.VMEM((Q_PART, LANES), BF), pltpu.VMEM((2, K_PART, LANES), BF),
            pltpu.VMEM((8192, LANES), BF),
            dma((6,)), dma((4,)), dma((NX,)), dma((NX,)), dma((NZ // 2,)), dma((2,)),
            dma((2,)), dma((2,)), dma((3,)),
        ],
        compiler_params=pltpu.CompilerParams(
            collective_id=0, has_side_effects=True, vmem_limit_bytes=40 * 2**20
        ),
        cost_estimate=pl.CostEstimate(
            flops=20 * Q_ALL * K_ALL * 64, bytes_accessed=2**20, transcendentals=2 * Q_ALL * K_ALL
        ),
        name="attention_backward",
    )(*[pltpu.with_memory_space_constraint(a, pltpu.HBM) for a in (query_saved, key_saved, value_saved, out_grad, log_norm, row_delta)])
    return pl.pallas_call(
        project,
        out_shape=(
            jax.ShapeDtypeStruct((Q_OWN, width), BF),
            jax.ShapeDtypeStruct((K_OWN, width), BF),
        ),
        in_specs=[vmem] * 5,
        out_specs=(vmem, vmem),
        compiler_params=pltpu.CompilerParams(vmem_limit_bytes=16 * 2**20),
        name="projections",
    )(full_q, full_kv, wq, wk, wv)


def solution(mesh):
    in_specs = (
        P(("pb", "ka"), None),
        P(("ka", "pb"), None),
        P(("ka", "pb"), None),
        P(("pb", "ka"), None),
        P(None, ("pb", "ka")),
        P(None, ("pb", "ka")),
        P(),
        P(),
        P(),
    )
    out_specs = (P(("pb", "ka"), None), P(("ka", "pb"), None))
    return jax.shard_map(local, mesh=mesh, in_specs=in_specs, out_specs=out_specs, check_vma=False)
```
